256 devices in a mesh: kv: 8 (over y, z_hi), seq: 32 (over x, z_lo, core).
Axes of the slice: x: 4, y: 4, z: 8 (z_hi: 2, z_lo: 4; z = z_hi * 4 + z_lo), core: 2. Of those that a mesh axis runs over, the one named last changes fastest.
Arguments:
- hidden: bfloat16 [8192, 8192], P('seq', 'kv'), may hold values from -12 to 12
- gain: bfloat16 [8192], P('kv'), may hold values from 0.5 to 4
- w_query: bfloat16 [8192, 4096], P('seq', 'kv')
- w_key: bfloat16 [8192, 1024], P('seq', 'kv')
- w_value: bfloat16 [8192, 1024], P('seq', 'kv'), may hold values from -0.0625 to 0.0625
- doc_ids: int32 [8192], P('seq'), may hold values from 0 to 16, as said below
Outputs:
- attended: bfloat16 [8192, 4096], P('seq', 'kv')
- cache: bfloat16 [2, 8192, 1024], P(None, 'seq', 'kv')
- lse: float32 [32, 8192], P('kv', 'seq')
The draws below stay inside these ranges and needn't reach their ends.
Inputs may be any that keep to these rules, and one draw needn't show every extreme that they name: `doc_ids`: numbers start at 0 and rise by one at each new document; there are 17 documents, exactly one of them holds 4096 tokens, and the 16 others hold 1 or more tokens each and 4096 tokens together.
All inputs are finite; a program needn't handle non-finite values.
Results may differ from the reference program's by a relative error of at most 0.006.
The reference program's roundings to bfloat16 on the way count: a program that leaves them out, or rounds other values in their place, can miss the bound.
Values may be sent and summed in bfloat16 or wider, within the bound.
A program may use at most 128 MiB of HBM per device.

```python
import jax
import jax.numpy as jnp
from jax import lax

D = 8192
HEAD = 128
QPK = 4
KV_HEADS = 8
Q_HEADS = 32
TOKENS = 8192
LONG = 4096


def query_base(key):
    return jax.random.normal(jax.random.fold_in(key, 11), (D, Q_HEADS * HEAD), jnp.float32) * D ** (-0.5)


def draw_hidden(key, part):
    noise_key = jax.random.fold_in(key, 0)
    values = jax.random.normal(noise_key, (TOKENS, D), jnp.float32)
    return jnp.clip(values, -12.0, 12.0).astype(jnp.bfloat16)


def draw_gain(key, part):
    values = jnp.exp(jax.random.uniform(key, (D,), jnp.float32, -0.69, 0.69))
    return jnp.clip(values, 0.5, 4.0).astype(jnp.bfloat16)


def draw_w_query(key, part):
    return query_base(key).astype(jnp.bfloat16)


def draw_w_key(key, part):
    noise = jax.random.normal(jax.random.fold_in(key, 23), (D, KV_HEADS * HEAD), jnp.float32) * D ** (-0.5)
    values = noise
    return values.astype(jnp.bfloat16)


def draw_doc_ids(key, part):
    cut_key = jax.random.fold_in(key, 31)
    slot_key = jax.random.fold_in(key, 37)
    shuffled = jax.random.permutation(cut_key, LONG - 1).astype(jnp.int32) + 1
    cuts = jnp.sort(shuffled[:15])
    bounds = jnp.concatenate([jnp.zeros((1,), jnp.int32), cuts, jnp.full((1,), LONG, jnp.int32)])
    slot = jax.random.randint(slot_key, (), 0, 17).astype(jnp.int32)
    order = jnp.arange(17, dtype=jnp.int32)
    earlier = jnp.concatenate([bounds[:1], bounds[:16]])
    starts = jnp.where(order <= slot, bounds, earlier + LONG)
    index = jnp.arange(TOKENS, dtype=jnp.int32)
    fresh = jnp.any(index[None, :] == starts[:, None], axis=0)
    return jnp.cumsum(fresh.astype(jnp.int32)).astype(jnp.int32) - 1


def block_levels(rng, shape, cuts, low, largest):
    factor_of = 1.0
    for axis_at, shards_of in cuts:
        steps = jax.random.uniform(jax.random.fold_in(jax.random.fold_in(rng, 6), axis_at), (shards_of,), jnp.float32, low / len(cuts), largest / len(cuts))
        factor_of = factor_of * jnp.repeat(jnp.exp(steps), shape[axis_at] // shards_of).reshape((-1,) + (1,) * (len(shape) - 1 - axis_at))
    return factor_of


def gaussian(rng, dims, scale, most, pieces=(), kind=jnp.bfloat16):
    values = jax.random.normal(rng, dims, jnp.float32) * scale
    if len(pieces) > 0:
        values = block_levels(rng, dims, pieces, -0.22, 0.18) * values
    return jnp.clip(values, min=-most, max=most).astype(kind)


def setup_inputs(seed: int = 0) -> dict:
    splits = jax.random.split(jax.random.key(seed), 7)
    return {
        "hidden": draw_hidden(jax.random.fold_in(splits[6], 71), 0),
        "gain": draw_gain(jax.random.fold_in(splits[6], 71), 0),
        "w_query": draw_w_query(jax.random.fold_in(splits[6], 71), 0),
        "w_key": draw_w_key(jax.random.fold_in(splits[6], 71), 0),
        "w_value": gaussian(splits[4], (D, KV_HEADS * HEAD), D ** -0.5, 0.0625, ((0, 32), (1, 8))),
        "doc_ids": draw_doc_ids(jax.random.fold_in(splits[6], 71), 0),
    }


eps = 1e-05
log_theta = 13.122363377404328

def doc_starts(ids):
    count = ids.shape[0]
    index = jnp.arange(count, dtype=jnp.int32)
    prior = jnp.concatenate([ids[:1] - 1, ids[:-1]])
    first = jnp.where(ids != prior, index, jnp.zeros_like(index))
    return lax.cummax(first, axis=0)

def rotate(values, positions):
    width = values.shape[-1]
    half = width // 2
    freq = jnp.exp(jnp.arange(half, dtype=jnp.float32) * (-2.0 * log_theta / width))
    angle = positions.astype(jnp.float32)[:, None] * freq[None, :]
    cosine = jnp.concatenate([jnp.cos(angle), jnp.cos(angle)], axis=-1)[:, None, :]
    sine = jnp.concatenate([jnp.sin(angle), jnp.sin(angle)], axis=-1)[:, None, :]
    turned = jnp.concatenate([-values[..., half:], values[..., :half]], axis=-1)
    return values * cosine + turned * sine

def normalize(rows, gain):
    wide = rows.astype(jnp.float32)
    factor = lax.rsqrt(lax.optimization_barrier(jnp.mean(wide * wide, axis=-1, keepdims=True)) + eps)
    return (wide * factor * gain.astype(jnp.float32)[None, :]).astype(jnp.bfloat16)

def reference(hidden, gain, w_query, w_key, w_value, doc_ids):
    normed = normalize(hidden, gain)
    key_index = jnp.arange(TOKENS, dtype=jnp.int32)
    positions = key_index - doc_starts(doc_ids)
    query = jnp.dot(normed, w_query, preferred_element_type=jnp.float32)
    query = rotate(query.reshape(TOKENS, Q_HEADS, HEAD), positions).astype(jnp.bfloat16)
    keys = jnp.dot(normed, w_key, preferred_element_type=jnp.float32)
    keys = rotate(keys.reshape(TOKENS, KV_HEADS, HEAD), positions).astype(jnp.bfloat16)
    values = jnp.dot(normed, w_value, preferred_element_type=jnp.float32).astype(jnp.bfloat16)
    values = values.reshape(TOKENS, KV_HEADS, HEAD)
    block = min(512, TOKENS)
    firsts = jnp.arange(TOKENS // block, dtype=jnp.int32) * block
    scale = HEAD ** (-0.5)
    outputs = []
    totals = []
    for group in range(KV_HEADS):
        group_q = query[:, group * QPK:(group + 1) * QPK, :]
        group_k = keys[:, group, :].astype(jnp.float32)
        group_v = values[:, group, :].astype(jnp.float32)

        def one_block(first):
            rows_q = lax.dynamic_slice_in_dim(group_q, first, block, 0).astype(jnp.float32)
            row_index = first + jnp.arange(block, dtype=jnp.int32)
            row_ids = lax.dynamic_slice_in_dim(doc_ids, first, block, 0)
            scores = jnp.einsum('bhd,td->hbt', rows_q, group_k) * scale
            seen = (key_index[None, :] <= row_index[:, None]) & (doc_ids[None, :] == row_ids[:, None])
            scores = jnp.where(seen[None], scores, -1e+30)
            best = lax.optimization_barrier(jnp.max(scores, axis=-1))
            weights = jnp.where(seen[None], jnp.exp(scores - best[..., None]), 0.0)
            total = lax.optimization_barrier(jnp.sum(weights, axis=-1))
            rounded = lax.optimization_barrier(weights.astype(jnp.bfloat16)).astype(jnp.float32)
            mixed = jnp.einsum('hbt,td->bhd', rounded, group_v) / jnp.transpose(total)[:, :, None]
            return (mixed.astype(jnp.bfloat16), best + jnp.log(total))
        mixed, sums = lax.map(one_block, firsts)
        outputs.append(mixed.reshape(TOKENS, QPK * HEAD))
        totals.append(jnp.transpose(sums, (1, 0, 2)).reshape(QPK, TOKENS))
    attended = jnp.concatenate(outputs, axis=1)
    lse = jnp.concatenate(totals, axis=0)
    cache = jnp.stack([keys.reshape(TOKENS, KV_HEADS * HEAD), values.reshape(TOKENS, KV_HEADS * HEAD)])
    return (attended, cache, lse)
```

```python
import functools

import jax
import jax.numpy as jnp
import numpy as np
from jax import lax
from jax.experimental import pallas as pl
from jax.experimental.pallas import tpu as pltpu
from jax.sharding import PartitionSpec as P

eps = 1e-05
log_theta = 13.122363377404328
MESH = pl.DeviceIdType.MESH
NX, NZ, NY, NH = 4, 4, 4, 2
DOCS = 17


def fused(
    hid_in, gain_in, wq_in, wk_in, wv_in, ids_in, freq_in,
    att_out, cache_out, lse_out,
    hbuf, rbuf, nbuf, wbuf, kvbuf, ibuf, gbuf, acc, qbuf, cosb, sinb, startb, m_ref, l_ref, o_ref,
    loc_sem, small_s, small_r, hz_s, hz_r, hy_s, hy_r,
    wz_s, wz_r, wx_s, wx_r, wc_s, wc_r,
    kz_s, kz_r, kx_s, kx_r, kc_s, kc_r,
):
    kv = lax.axis_index("kv")
    seq = lax.axis_index("seq")
    y, zhi = kv // 2, kv % 2
    c = seq % 2
    zlo = (seq // 2) % 4
    x = seq // 8
    zz = zhi * 4 + zlo

    def at(x_=None, y_=None, zlo_=None, zhi_=None, c_=None):
        x_ = x if x_ is None else x_
        y_ = y if y_ is None else y_
        zlo_ = zlo if zlo_ is None else zlo_
        zhi_ = zhi if zhi_ is None else zhi_
        c_ = c if c_ is None else c_
        return (y_ * 2 + zhi_, (x_ * 4 + zlo_) * 2 + c_)

    def ring_z(step):
        z_ = (zz + 8 + step) % 8
        return z_ % 4, z_ // 4

    xp, xm, xo = (x + 1) % 4, (x + 3) % 4, (x + 2) % 4
    yp, ym, yo = (y + 1) % 4, (y + 3) % 4, (y + 2) % 4
    up_lo, up_hi = ring_z(2)
    dn_lo, dn_hi = ring_z(-2)
    sib = at(c_=1 - c)
    dev_xp, dev_xm = at(x_=xp), at(x_=xm)
    dev_yp, dev_ym = at(y_=yp), at(y_=ym)
    dev_up2, dev_dn2 = at(zlo_=up_lo, zhi_=up_hi), at(zlo_=dn_lo, zhi_=dn_hi)
    dev_zu, dev_zd = at(zlo_=(zlo + 1) % 4), at(zlo_=(zlo + 3) % 4)
    dev_pair = at(zhi_=1 - zhi)

    def rc(src, dst, ss, rs, dev):
        return pltpu.make_async_remote_copy(
            src_ref=src, dst_ref=dst, send_sem=ss, recv_sem=rs, device_id=dev, device_id_type=MESH
        )

    sent = []

    def send(src, dst, ss, rs, dev):
        d = rc(src, dst, ss, rs, dev)
        d.start()
        sent.append((None, d))

    def send_if(cond, src, dst, ss, rs, dev):
        d = rc(src, dst, ss, rs, dev)

        @pl.when(cond)
        def _():
            d.start()

        sent.append((cond, d))

    def got(ref, ss, rs):
        rc(ref, ref, ss, rs, sib).wait_recv()

    wmine = wbuf.at[c, x, zlo]
    hmine = hbuf.at[kv]
    locals_ = [
        pltpu.make_async_copy(wq_in, wmine.at[:, :, pl.ds(0, 512)], loc_sem.at[0]),
        pltpu.make_async_copy(wk_in, wmine.at[:, :, pl.ds(512, 128)], loc_sem.at[1]),
        pltpu.make_async_copy(wv_in, wmine.at[:, :, pl.ds(640, 128)], loc_sem.at[2]),
        pltpu.make_async_copy(hid_in, hmine, loc_sem.at[3]),
        pltpu.make_async_copy(ids_in, ibuf.at[c, x, zlo], loc_sem.at[4]),
        pltpu.make_async_copy(gain_in, gbuf.at[y, zhi], loc_sem.at[5]),
    ]
    for d in locals_:
        d.start()

    barrier = pltpu.get_barrier_semaphore()
    peers = [sib, dev_pair, dev_up2, dev_dn2]
    for d in (1, 2, 3):
        peers += [at(x_=(x + d) % 4), at(y_=(y + d) % 4), at(zlo_=(zlo + d) % 4)]
    for dev in peers:
        pl.semaphore_signal(barrier, inc=1, device_id=dev, device_id_type=MESH)
    for d in locals_:
        d.wait()
    pl.semaphore_wait(barrier, len(peers))

    for d in (1, 2, 3):
        t = ibuf.at[c, x, zlo]
        send(t, t, small_s.at[d - 1], small_r.at[d - 1], at(zlo_=(zlo + d) % 4))
    t = gbuf.at[y, zhi]
    send(t, t, small_s.at[3], small_r.at[3], dev_pair)

    class Gather:
        def __init__(self, buf, zs, zr, xs, xr, cs, cr):
            self.buf, self.zs, self.zr, self.xs, self.xr, self.cs, self.cr = buf, zs, zr, xs, xr, cs, cr

        def block(self, r):
            if r == 0:
                return zlo
            mid = {1: (0, 3), 2: (2, 1), 3: (3, 0)}[r]
            return jnp.where(
                zlo == 0, r, jnp.where(zlo == 3, 3 - r, jnp.where(zlo == 1, mid[0], mid[1]))
            )

        def to_sib(self, x_, b):
            s = self.buf.at[c, x_, b]
            send(s, s, self.cs.at[x_, b], self.cr.at[x_, b], sib)

        def z_step(self, r):
            b = self.block(r)
            s = self.buf.at[c, x, b]
            if r > 0:
                got(s, self.zs.at[0, b], self.zr.at[b])
            send_if((zlo < 3) & (b <= zlo), s, s, self.zs.at[0, b], self.zr.at[b], dev_zu)
            send_if((zlo > 0) & (b >= zlo), s, s, self.zs.at[1, b], self.zr.at[b], dev_zd)
            send(s, s, self.xs.at[0, b], self.xr.at[0, b], dev_xp)
            send(s, s, self.xs.at[1, b], self.xr.at[1, b], dev_xm)
            self.to_sib(x, b)

        def x_step(self, r):
            b = self.block(r)
            s = self.buf.at[c, xm, b]
            got(s, self.xs.at[0, b], self.xr.at[0, b])
            h = s.at[0]
            send(h, h, self.xs.at[2, b], self.xr.at[2, b], dev_xp)
            s2 = self.buf.at[c, xp, b]
            got(s2, self.xs.at[1, b], self.xr.at[1, b])
            h = s2.at[1]
            send(h, h, self.xs.at[3, b], self.xr.at[3, b], dev_xm)
            self.to_sib(xm, b)
            self.to_sib(xp, b)

        def opp_step(self, r):
            b = self.block(r)
            s = self.buf.at[c, xo, b]
            got(s.at[0], self.xs.at[2, b], self.xr.at[2, b])
            got(s.at[1], self.xs.at[3, b], self.xr.at[3, b])
            self.to_sib(xo, b)

        def sib_wait(self, x_, r):
            b = self.block(r)
            got(self.buf.at[1 - c, x_, b], self.cs.at[x_, b], self.cr.at[x_, b])

    W = Gather(wbuf, wz_s, wz_r, wx_s, wx_r, wc_s, wc_r)
    KV = Gather(kvbuf, kz_s, kz_r, kx_s, kx_r, kc_s, kc_r)

    def y_send(g, zh):
        s = hbuf.at[y * 2 + zh]
        send(s, s, hy_s.at[g, 0], hy_r.at[g, 0], dev_yp)
        send(s, s, hy_s.at[g, 1], hy_r.at[g, 1], dev_ym)

    def y_fwd(g, zh):
        s = hbuf.at[ym * 2 + zh]
        got(s, hy_s.at[g, 0], hy_r.at[g, 0])
        send(s.at[0], s.at[0], hy_s.at[g, 2], hy_r.at[g, 2], dev_yp)
        s = hbuf.at[yp * 2 + zh]
        got(s, hy_s.at[g, 1], hy_r.at[g, 1])
        send(s.at[1], s.at[1], hy_s.at[g, 3], hy_r.at[g, 3], dev_ym)

    def y_end(g, zh):
        s = hbuf.at[yo * 2 + zh]
        got(s.at[0], hy_s.at[g, 2], hy_r.at[g, 2])
        got(s.at[1], hy_s.at[g, 3], hy_r.at[g, 3])

    W.z_step(0)
    send(hmine.at[0], rbuf.at[0], hz_s.at[0], hz_r.at[0], dev_up2)
    send(hmine.at[1], rbuf.at[1], hz_s.at[1], hz_r.at[1], dev_dn2)
    y_send(0, zhi)

    for d in (1, 2, 3):
        got(ibuf.at[c, x, (zlo + 4 - d) % 4], small_s.at[d - 1], small_r.at[d - 1])
    got(gbuf.at[y, 1 - zhi], small_s.at[3], small_r.at[3])
    for d in (1, 2, 3):
        t = ibuf.at[c, x]
        send(t, t, small_s.at[3 + d], small_r.at[3 + d], at(x_=(x + d) % 4))
        t = gbuf.at[y]
        send(t, t, small_s.at[6 + d], small_r.at[6 + d], at(y_=(y + d) % 4))
    for d in (1, 2, 3):
        got(ibuf.at[c, (x + 4 - d) % 4], small_s.at[3 + d], small_r.at[3 + d])
        got(gbuf.at[(y + 4 - d) % 4], small_s.at[6 + d], small_r.at[6 + d])
    t = ibuf.at[c]
    send(t, t, small_s.at[10], small_r.at[10], sib)
    got(ibuf.at[1 - c], small_s.at[10], small_r.at[10])

    every = ibuf[...].reshape(32, 8, 128)
    mine = ibuf[c, x, zlo].astype(jnp.float32)
    idc = jnp.concatenate(
        [jnp.transpose(jnp.broadcast_to(mine[i : i + 1, :], (128, 128))) for i in (0, 1)], axis=0
    )
    start = jnp.zeros((256, 128), jnp.float32)
    for d in range(DOCS - 1):
        hits = jnp.sum(jnp.where(every == d, 1.0, 0.0), axis=0)
        total = jnp.sum(jnp.sum(hits, axis=0, keepdims=True), axis=1, keepdims=True)
        start = start + jnp.where(idc > d, total, 0.0)
    startb[...] = start
    row = lax.broadcasted_iota(jnp.int32, (256, 128), 0).astype(jnp.float32)
    tok = row + (seq * 256).astype(jnp.float32)
    angle = (tok - start) * freq_in[0:1, :]
    lane = lax.broadcasted_iota(jnp.int32, (256, 128), 1)
    cosb[...] = jnp.cos(angle)
    sinb[...] = jnp.where(lane < 64, -1.0, 1.0) * jnp.sin(angle)

    W.x_step(0)
    W.z_step(1)
    got(rbuf.at[0], hz_s.at[0], hz_r.at[0])
    send(rbuf.at[0], hbuf.at[y * 2 + dn_hi, 0], hz_s.at[2], hz_r.at[2], dev_up2)
    got(rbuf.at[1], hz_s.at[1], hz_r.at[1])
    send(rbuf.at[1], hbuf.at[y * 2 + up_hi, 1], hz_s.at[3], hz_r.at[3], dev_dn2)
    y_fwd(0, zhi)
    W.x_step(1)
    W.z_step(2)
    got(hbuf.at[y * 2 + 1 - zhi, 0], hz_s.at[2], hz_r.at[2])
    got(hbuf.at[y * 2 + 1 - zhi, 1], hz_s.at[3], hz_r.at[3])
    y_send(1, 1 - zhi)
    W.opp_step(0)
    W.x_step(2)
    W.z_step(3)
    y_end(0, zhi)
    y_fwd(1, 1 - zhi)
    W.opp_step(1)
    y_end(1, 1 - zhi)

    def squares(k, total):
        for i in range(8):
            h = hbuf[k, :, :, i * 128 : (i + 1) * 128].reshape(256, 128).astype(jnp.float32)
            total = total + h * h
        return total

    total = lax.fori_loop(0, 8, squares, jnp.zeros((256, 128), jnp.float32))
    factor = lax.rsqrt(jnp.sum(total, axis=1, keepdims=True) * (1.0 / 8192.0) + eps)
    factor = jnp.broadcast_to(factor, (256, 128))

    @pl.loop(0, 8)
    def _(k):
        g = gbuf[k // 2, k % 2]
        for i in range(8):
            h = hbuf[k, :, :, i * 128 : (i + 1) * 128].reshape(256, 128).astype(jnp.float32)
            nbuf[k * 4 + i // 2, :, (i % 2) * 128 : (i % 2 + 1) * 128] = (
                h * factor * g[i : i + 1, :]
            ).astype(jnp.bfloat16)

    W.x_step(3)
    W.opp_step(2)

    acc[...] = jnp.zeros_like(acc)

    def multiply(r):
        b = W.block(r)

        @pl.loop(0, 8)
        def _(i):
            x_, c_ = i // 2, i % 2
            w = wbuf[c_, x_, b].reshape(256, 768)
            acc[...] += jnp.dot(nbuf[(x_ * 4 + b) * 2 + c_], w, preferred_element_type=jnp.float32)

    for r in range(4):
        if r == 3:
            W.opp_step(3)
        for x_ in (x, xm, xp, xo):
            W.sib_wait(x_, r)
        multiply(r)

    def turn(u):
        return u * cosb[...] + pltpu.roll(u, 64, 1) * sinb[...]

    kmine = turn(acc[:, 512:640]).astype(jnp.bfloat16)
    vmine = acc[:, 640:768].astype(jnp.bfloat16)
    kvbuf[c, x, zlo, 0] = kmine
    kvbuf[c, x, zlo, 1] = vmine
    cache_out[0] = kmine
    cache_out[1] = vmine
    for h in range(4):
        qbuf[h] = turn(acc[:, h * 128 : (h + 1) * 128]).astype(jnp.bfloat16)
    KV.z_step(0)

    scale = 128 ** (-0.5)
    lane_f = lax.broadcasted_iota(jnp.int32, (1, 512), 1).astype(jnp.float32)

    def chunk(x_, b, first):
        base = ((x_ * 4 + b) * 512).astype(jnp.float32)
        keys = kvbuf[:, x_, b, 0].reshape(512, 128)
        vals = kvbuf[:, x_, b, 1].reshape(512, 128)
        low = startb[:, 0:1] - base
        seen = lane_f >= low
        if first:
            here = (
                lax.broadcasted_iota(jnp.int32, (256, 1), 0).astype(jnp.float32)
                + (c * 256).astype(jnp.float32)
            )
            seen = seen & (lane_f <= here)
        for h in range(4):
            s = lax.dot_general(
                qbuf[h], keys, (((1,), (1,)), ((), ())), preferred_element_type=jnp.float32
            )
            s = jnp.where(seen, s * scale, -1e30)
            top = jnp.max(s, axis=1, keepdims=True)
            if first:
                new = jnp.broadcast_to(top, (256, 128))
            else:
                old = m_ref[h]
                new = jnp.maximum(old, top)
            p = jnp.exp(s - new[:, 0:1])
            total = jnp.sum(p, axis=1, keepdims=True)
            part = jnp.dot(p.astype(jnp.bfloat16), vals, preferred_element_type=jnp.float32)
            if first:
                l_ref[h] = jnp.broadcast_to(total, (256, 128))
                o_ref[h] = part
            else:
                alpha = jnp.exp(old - new)
                l_ref[h] = l_ref[h] * alpha + total
                o_ref[h] = o_ref[h] * alpha + part
            m_ref[h] = new

    def chunk_if(cond, x_, b):
        @pl.when(cond)
        def _():
            chunk(x_, b, False)

    KV.sib_wait(x, 0)
    chunk(x, zlo, True)
    KV.x_step(0)
    KV.z_step(1)
    KV.sib_wait(x, 1)
    chunk_if(KV.block(1) < zlo, x, KV.block(1))
    KV.x_step(1)
    KV.z_step(2)
    KV.opp_step(0)
    KV.sib_wait(x, 2)
    chunk_if(KV.block(2) < zlo, x, KV.block(2))
    KV.x_step(2)
    KV.z_step(3)
    KV.opp_step(1)
    KV.sib_wait(x, 3)
    chunk_if(KV.block(3) < zlo, x, KV.block(3))
    KV.x_step(3)
    KV.opp_step(2)
    for r in range(4):
        KV.sib_wait(xm, r)
        KV.sib_wait(xp, r)

    @pl.when(x >= 1)
    def _():
        @pl.loop(0, 4)
        def _(b):
            chunk(x - 1, b, False)

    KV.opp_step(3)
    for r in range(4):
        KV.sib_wait(xo, r)

    @pl.when(x >= 2)
    def _():
        @pl.loop(zlo, 4)
        def _(b):
            chunk(x - 2, b, False)

    for h in range(4):
        att_out[:, h * 128 : (h + 1) * 128] = (o_ref[h] / l_ref[h]).astype(jnp.bfloat16)
        logs = m_ref[h] + jnp.log(l_ref[h])
        for i in (0, 1):
            lse_out[h : h + 1, i * 128 : (i + 1) * 128] = jnp.transpose(
                logs[i * 128 : (i + 1) * 128, :]
            )[0:1, :]

    for cond, d in sent:
        if cond is None:
            d.wait_send()
        else:
            @pl.when(cond)
            def _(d=d):
                d.wait_send()


def on_device(hidden, gain, w_query, w_key, w_value, doc_ids):
    bf, f32 = jnp.bfloat16, jnp.float32
    hid = hidden.reshape(2, 128, 1024)
    tile = jnp.concatenate([doc_ids.reshape(2, 128), jnp.full((6, 128), 1 << 20, jnp.int32)], axis=0)
    gains = gain.astype(f32).reshape(8, 128)
    freq = np.exp(np.arange(64, dtype=np.float32) * np.float32(-2.0 * log_theta / 128))
    freq = jnp.asarray(np.tile(np.concatenate([freq, freq])[None], (8, 1)).astype(np.float32))
    dma = pltpu.SemaphoreType.DMA
    any_, vm = pl.BlockSpec(memory_space=pl.ANY), pl.BlockSpec(memory_space=pltpu.VMEM)
    mixed, cache, sums = pl.pallas_call(
        fused,
        out_shape=(
            jax.ShapeDtypeStruct((256, 512), bf),
            jax.ShapeDtypeStruct((2, 256, 128), bf),
            jax.ShapeDtypeStruct((4, 256), f32),
        ),
        in_specs=[any_] * 6 + [vm],
        out_specs=(vm, vm, vm),
        scratch_shapes=[
            pltpu.VMEM((8, 2, 128, 1024), bf),
            pltpu.VMEM((2, 128, 1024), bf),
            pltpu.VMEM((32, 256, 256), bf),
            pltpu.VMEM((2, 4, 4, 2, 128, 768), bf),
            pltpu.VMEM((2, 4, 4, 2, 256, 128), bf),
            pltpu.VMEM((2, 4, 4, 8, 128), jnp.int32),
            pltpu.VMEM((4, 2, 8, 128), f32),
            pltpu.VMEM((256, 768), f32),
            pltpu.VMEM((4, 256, 128), bf),
            pltpu.VMEM((256, 128), f32),
            pltpu.VMEM((256, 128), f32),
            pltpu.VMEM((256, 128), f32),
            pltpu.VMEM((4, 256, 128), f32),
            pltpu.VMEM((4, 256, 128), f32),
            pltpu.VMEM((4, 256, 128), f32),
            dma((6,)), dma((11,)), dma((11,)), dma((4,)), dma((4,)), dma((2, 4)), dma((2, 4)),
        ]
        + [dma((2, 4)), dma((4,)), dma((4, 4)), dma((4, 4)), dma((4, 4)), dma((4, 4))] * 2,
        compiler_params=pltpu.CompilerParams(
            collective_id=0, has_side_effects=True, vmem_limit_bytes=62 * 1024 * 1024
        ),
        name="fused",
    )(
        hid, gains, w_query.reshape(2, 128, 512), w_key.reshape(2, 128, 128),
        w_value.reshape(2, 128, 128), tile, freq,
    )
    return mixed, cache, sums


def solution(mesh):
    in_specs = (P("seq", "kv"), P("kv"), P("seq", "kv"), P("seq", "kv"), P("seq", "kv"), P("seq"))
    out_specs = (P("seq", "kv"), P(None, "seq", "kv"), P("kv", "seq"))
    return jax.shard_map(
        on_device, mesh=mesh, in_specs=in_specs, out_specs=out_specs, check_vma=False
    )
```

```python
import functools

import jax
import jax.numpy as jnp
import numpy as np
from jax import lax
from jax.experimental import pallas as pl
from jax.experimental.pallas import tpu as pltpu
from jax.sharding import PartitionSpec as P

eps = 1e-05
log_theta = 13.122363377404328
MESH = pl.DeviceIdType.MESH
NX, NZ, NY, NH = 4, 4, 4, 2
DOCS = 17


def fused(
    hid_in, gain_in, wq_in, wk_in, wv_in, ids_in, freq_in,
    att_out, cache_out, lse_out,
    hbuf, rbuf, nbuf, wbuf, kvbuf, ibuf, gbuf, acc, qbuf, cosb, sinb, startb, m_ref, l_ref, o_ref,
    loc_sem, small_s, small_r, hz_s, hz_r, hy_s, hy_r, hf_s, hf_r,
    wz_s, wz_r, wx_s, wx_r, wf_s, wf_r, wc_s, wc_r,
    kz_s, kz_r, kx_s, kx_r, kf_s, kf_r, kc_s, kc_r,
):
    kv = lax.axis_index("kv")
    seq = lax.axis_index("seq")
    y, zhi = kv // 2, kv % 2
    c = seq % 2
    zlo = (seq // 2) % 4
    x = seq // 8
    zz = zhi * 4 + zlo

    def at(x_=None, y_=None, zlo_=None, zhi_=None, c_=None):
        x_ = x if x_ is None else x_
        y_ = y if y_ is None else y_
        zlo_ = zlo if zlo_ is None else zlo_
        zhi_ = zhi if zhi_ is None else zhi_
        c_ = c if c_ is None else c_
        return (y_ * 2 + zhi_, (x_ * 4 + zlo_) * 2 + c_)

    def ring_z(step):
        z_ = (zz + 8 + step) % 8
        return z_ % 4, z_ // 4

    xp, xm, xo = (x + 1) % 4, (x + 3) % 4, (x + 2) % 4
    yp, ym, yo = (y + 1) % 4, (y + 3) % 4, (y + 2) % 4
    up_lo, up_hi = ring_z(2)
    dn_lo, dn_hi = ring_z(-2)
    sib = at(c_=1 - c)
    dev_xp, dev_xm = at(x_=xp), at(x_=xm)
    dev_yp, dev_ym = at(y_=yp), at(y_=ym)
    dev_up2, dev_dn2 = at(zlo_=up_lo, zhi_=up_hi), at(zlo_=dn_lo, zhi_=dn_hi)
    dev_zu, dev_zd = at(zlo_=(zlo + 1) % 4), at(zlo_=(zlo + 3) % 4)
    dev_pair = at(zhi_=1 - zhi)

    def rc(src, dst, ss, rs, dev):
        return pltpu.make_async_remote_copy(
            src_ref=src, dst_ref=dst, send_sem=ss, recv_sem=rs, device_id=dev, device_id_type=MESH
        )

    sent = []

    def send(src, dst, ss, rs, dev):
        d = rc(src, dst, ss, rs, dev)
        d.start()
        sent.append((None, d))

    def send_if(cond, src, dst, ss, rs, dev):
        d = rc(src, dst, ss, rs, dev)

        @pl.when(cond)
        def _():
            d.start()

        sent.append((cond, d))

    def got(ref, ss, rs):
        rc(ref, ref, ss, rs, sib).wait_recv()

    wmine = wbuf.at[c, x, zlo]
    hmine = hbuf.at[kv]
    locals_ = [
        pltpu.make_async_copy(wq_in, wmine.at[:, :, pl.ds(0, 512)], loc_sem.at[0]),
        pltpu.make_async_copy(wk_in, wmine.at[:, :, pl.ds(512, 128)], loc_sem.at[1]),
        pltpu.make_async_copy(wv_in, wmine.at[:, :, pl.ds(640, 128)], loc_sem.at[2]),
        pltpu.make_async_copy(hid_in, hmine, loc_sem.at[3]),
        pltpu.make_async_copy(ids_in, ibuf.at[c, x, zlo], loc_sem.at[4]),
        pltpu.make_async_copy(gain_in, gbuf.at[y, zhi], loc_sem.at[5]),
    ]
    for d in locals_:
        d.start()

    barrier = pltpu.get_barrier_semaphore()
    peers = [sib, dev_pair, dev_up2, dev_dn2]
    for d in (1, 2, 3):
        peers += [at(x_=(x + d) % 4), at(y_=(y + d) % 4), at(zlo_=(zlo + d) % 4)]
    for dev in peers:
        pl.semaphore_signal(barrier, inc=1, device_id=dev, device_id_type=MESH)
    for d in locals_:
        d.wait()
    pl.semaphore_wait(barrier, len(peers))

    for d in (1, 2, 3):
        t = ibuf.at[c, x, zlo]
        send(t, t, small_s.at[d - 1], small_r.at[d - 1], at(zlo_=(zlo + d) % 4))
    t = gbuf.at[y, zhi]
    send(t, t, small_s.at[3], small_r.at[3], dev_pair)

    class Gather:
        def __init__(self, buf, zs, zr, xs, xr, fs, fr, cs, cr):
            self.buf, self.zs, self.zr, self.xs, self.xr = buf, zs, zr, xs, xr
            self.fs, self.fr, self.cs, self.cr = fs, fr, cs, cr

        def block(self, r):
            if r == 0:
                return zlo
            mid = {1: (0, 3), 2: (2, 1), 3: (3, 0)}[r]
            return jnp.where(
                zlo == 0, r, jnp.where(zlo == 3, 3 - r, jnp.where(zlo == 1, mid[0], mid[1]))
            )

        def to_sib(self, x_, b):
            s = self.buf.at[c, x_, b]
            send(s, s, self.cs.at[x_, b], self.cr.at[x_, b], sib)

        def z_part(self, b, h):
            s = self.buf.at[c, x, b, h]
            send_if((zlo < 3) & (b <= zlo), s, s, self.zs.at[0, b, h], self.zr.at[b, h], dev_zu)
            send_if((zlo > 0) & (b >= zlo), s, s, self.zs.at[1, b, h], self.zr.at[b, h], dev_zd)

        def x_part(self, b, h, way):
            s = self.buf.at[c, x, b, h]
            send(s, s, self.xs.at[way, b, h], self.xr.at[way, b, h], (dev_xp, dev_xm)[way])

        def first(self):
            for h in (0, 1):
                self.z_part(zlo, h)
                self.x_part(zlo, h, 0)
                self.x_part(zlo, 1 - h, 1)
            self.to_sib(x, zlo)

        def z_step(self, r, h):
            b = self.block(r)
            got(self.buf.at[c, x, b, h], self.zs.at[0, b, h], self.zr.at[b, h])
            self.z_part(b, h)
            self.x_part(b, h, 0)
            self.x_part(b, h, 1)
            if h == 1:
                self.to_sib(x, b)

        def x_fwd(self, r):
            b = self.block(r)
            t = self.buf.at[c, xm, b, 0]
            got(t, self.xs.at[0, b, 0], self.xr.at[0, b, 0])
            send(t, t, self.fs.at[0, b], self.fr.at[0, b], dev_xp)
            t = self.buf.at[c, xp, b, 1]
            got(t, self.xs.at[1, b, 1], self.xr.at[1, b, 1])
            send(t, t, self.fs.at[1, b], self.fr.at[1, b], dev_xm)

        def x_rest(self, r):
            b = self.block(r)
            got(self.buf.at[c, xm, b, 1], self.xs.at[0, b, 1], self.xr.at[0, b, 1])
            self.to_sib(xm, b)
            got(self.buf.at[c, xp, b, 0], self.xs.at[1, b, 0], self.xr.at[1, b, 0])
            self.to_sib(xp, b)

        def opp_step(self, r):
            b = self.block(r)
            t = self.buf.at[c, xo, b]
            got(t.at[0], self.fs.at[0, b], self.fr.at[0, b])
            got(t.at[1], self.fs.at[1, b], self.fr.at[1, b])
            self.to_sib(xo, b)

        def sib_wait(self, x_, r):
            b = self.block(r)
            got(self.buf.at[1 - c, x_, b], self.cs.at[x_, b], self.cr.at[x_, b])

    W = Gather(wbuf, wz_s, wz_r, wx_s, wx_r, wf_s, wf_r, wc_s, wc_r)
    KV = Gather(kvbuf, kz_s, kz_r, kx_s, kx_r, kf_s, kf_r, kc_s, kc_r)

    def y_part(g, zh, h, way):
        t = hbuf.at[y * 2 + zh, h]
        send(t, t, hy_s.at[g, way, h], hy_r.at[g, way, h], (dev_yp, dev_ym)[way])

    def y_fwd(g, zh):
        t = hbuf.at[ym * 2 + zh, 0]
        got(t, hy_s.at[g, 0, 0], hy_r.at[g, 0, 0])
        send(t, t, hf_s.at[g, 0], hf_r.at[g, 0], dev_yp)
        t = hbuf.at[yp * 2 + zh, 1]
        got(t, hy_s.at[g, 1, 1], hy_r.at[g, 1, 1])
        send(t, t, hf_s.at[g, 1], hf_r.at[g, 1], dev_ym)

    def y_end(g, zh):
        got(hbuf.at[ym * 2 + zh, 1], hy_s.at[g, 0, 1], hy_r.at[g, 0, 1])
        got(hbuf.at[yp * 2 + zh, 0], hy_s.at[g, 1, 0], hy_r.at[g, 1, 0])
        for h in (0, 1):
            got(hbuf.at[yo * 2 + zh, h], hf_s.at[g, h], hf_r.at[g, h])

    quarter = [pl.ds(0, 64), pl.ds(64, 64)]

    def relay(p):
        for way, hi, dev in ((0, dn_hi, dev_up2), (1, up_hi, dev_dn2)):
            t = rbuf.at[way, quarter[p]]
            got(t, hz_s.at[0, way, p], hz_r.at[0, way, p])
            send(
                t, hbuf.at[y * 2 + hi, way, quarter[p]],
                hz_s.at[1, way, p], hz_r.at[1, way, p], dev,
            )

    W.first()
    for p in (0, 1):
        for way, dev in ((0, dev_up2), (1, dev_dn2)):
            send(
                hmine.at[way, quarter[p]], rbuf.at[way, quarter[p]],
                hz_s.at[0, way, p], hz_r.at[0, way, p], dev,
            )
    for h in (0, 1):
        y_part(0, zhi, h, 0)
        y_part(0, zhi, 1 - h, 1)

    def small_two():
        for d in (1, 2, 3):
            got(ibuf.at[c, x, (zlo + 4 - d) % 4], small_s.at[d - 1], small_r.at[d - 1])
        got(gbuf.at[y, 1 - zhi], small_s.at[3], small_r.at[3])
        for d in (1, 2, 3):
            t = ibuf.at[c, x]
            send(t, t, small_s.at[3 + d], small_r.at[3 + d], at(x_=(x + d) % 4))
            t = gbuf.at[y]
            send(t, t, small_s.at[6 + d], small_r.at[6 + d], at(y_=(y + d) % 4))

    def small_three():
        for d in (1, 2, 3):
            got(ibuf.at[c, (x + 4 - d) % 4], small_s.at[3 + d], small_r.at[3 + d])
            got(gbuf.at[(y + 4 - d) % 4], small_s.at[6 + d], small_r.at[6 + d])
        t = ibuf.at[c]
        send(t, t, small_s.at[10], small_r.at[10], sib)

    def squares(zh, total):
        def one(i, total):
            for j in range(8):
                h = hbuf[i * 2 + zh, :, :, j * 128 : (j + 1) * 128].reshape(256, 128)
                h = h.astype(jnp.float32)
                total = total + h * h
            return total

        return lax.fori_loop(0, 4, one, total)

    W.x_fwd(0)
    W.z_step(1, 0)
    W.z_step(1, 1)
    y_fwd(0, zhi)
    W.x_rest(0)
    relay(0)
    small_two()
    W.x_fwd(1)
    relay(1)
    W.z_step(2, 0)
    W.opp_step(0)
    W.x_rest(1)
    W.z_step(2, 1)
    small_three()
    y_end(0, zhi)
    W.x_fwd(2)
    for h in (0, 1):
        for p in (0, 1):
            t = hbuf.at[y * 2 + 1 - zhi, h, quarter[p]]
            got(t, hz_s.at[1, h, p], hz_r.at[1, h, p])
        y_part(1, 1 - zhi, h, 0)
        y_part(1, 1 - zhi, h, 1)
    W.opp_step(1)
    W.x_rest(2)
    got(ibuf.at[1 - c], small_s.at[10], small_r.at[10])

    every = ibuf[...].reshape(32, 8, 128)
    mine = ibuf[c, x, zlo].astype(jnp.float32)
    idc = jnp.concatenate(
        [jnp.transpose(jnp.broadcast_to(mine[i : i + 1, :], (128, 128))) for i in (0, 1)], axis=0
    )
    start = jnp.zeros((256, 128), jnp.float32)
    for d in range(DOCS - 1):
        hits = jnp.sum(jnp.where(every == d, 1.0, 0.0), axis=0)
        total = jnp.sum(jnp.sum(hits, axis=0, keepdims=True), axis=1, keepdims=True)
        start = start + jnp.where(idc > d, total, 0.0)
    startb[...] = start
    row = lax.broadcasted_iota(jnp.int32, (256, 128), 0).astype(jnp.float32)
    tok = row + (seq * 256).astype(jnp.float32)
    angle = (tok - start) * freq_in[0:1, :]
    lane = lax.broadcasted_iota(jnp.int32, (256, 128), 1)
    cosb[...] = jnp.cos(angle)
    sinb[...] = jnp.where(lane < 64, -1.0, 1.0) * jnp.sin(angle)

    W.z_step(3, 0)
    y_fwd(1, 1 - zhi)
    total = squares(zhi, jnp.zeros((256, 128), jnp.float32))
    W.z_step(3, 1)
    W.opp_step(2)
    W.x_fwd(3)
    y_end(1, 1 - zhi)

    total = squares(1 - zhi, total)
    factor = lax.rsqrt(jnp.sum(total, axis=1, keepdims=True) * (1.0 / 8192.0) + eps)
    factor = jnp.broadcast_to(factor, (256, 128))

    @pl.loop(0, 8)
    def _(k):
        g = gbuf[k // 2, k % 2]
        for i in range(8):
            h = hbuf[k, :, :, i * 128 : (i + 1) * 128].reshape(256, 128).astype(jnp.float32)
            nbuf[k * 4 + i // 2, :, (i % 2) * 128 : (i % 2 + 1) * 128] = (
                h * factor * g[i : i + 1, :]
            ).astype(jnp.bfloat16)

    W.x_rest(3)

    acc[...] = jnp.zeros_like(acc)

    def multiply(r):
        b = W.block(r)

        @pl.loop(0, 8)
        def _(i):
            x_, c_ = i // 2, i % 2
            w = wbuf[c_, x_, b].reshape(256, 768)
            acc[...] += jnp.dot(nbuf[(x_ * 4 + b) * 2 + c_], w, preferred_element_type=jnp.float32)

    for r in range(4):
        if r == 3:
            W.opp_step(3)
        for x_ in (x, xm, xp, xo):
            W.sib_wait(x_, r)
        multiply(r)

    def turn(u):
        return u * cosb[...] + pltpu.roll(u, 64, 1) * sinb[...]

    kmine = turn(acc[:, 512:640]).astype(jnp.bfloat16)
    vmine = acc[:, 640:768].astype(jnp.bfloat16)
    kvbuf[c, x, zlo, 0] = kmine
    kvbuf[c, x, zlo, 1] = vmine
    cache_out[0] = kmine
    cache_out[1] = vmine
    for h in range(4):
        qbuf[h] = turn(acc[:, h * 128 : (h + 1) * 128]).astype(jnp.bfloat16)
    KV.first()

    scale = 128 ** (-0.5)
    lane_f = lax.broadcasted_iota(jnp.int32, (1, 512), 1).astype(jnp.float32)

    def chunk(x_, b, first):
        base = ((x_ * 4 + b) * 512).astype(jnp.float32)
        keys = kvbuf[:, x_, b, 0].reshape(512, 128)
        vals = kvbuf[:, x_, b, 1].reshape(512, 128)
        low = startb[:, 0:1] - base
        seen = lane_f >= low
        if first:
            here = (
                lax.broadcasted_iota(jnp.int32, (256, 1), 0).astype(jnp.float32)
                + (c * 256).astype(jnp.float32)
            )
            seen = seen & (lane_f <= here)
        for h in range(4):
            s = lax.dot_general(
                qbuf[h], keys, (((1,), (1,)), ((), ())), preferred_element_type=jnp.float32
            )
            s = jnp.where(seen, s * scale, -1e30)
            top = jnp.max(s, axis=1, keepdims=True)
            if first:
                new = jnp.broadcast_to(top, (256, 128))
            else:
                old = m_ref[h]
                new = jnp.maximum(old, top)
            p = jnp.exp(s - new[:, 0:1])
            total = jnp.sum(p, axis=1, keepdims=True)
            part = jnp.dot(p.astype(jnp.bfloat16), vals, preferred_element_type=jnp.float32)
            if first:
                l_ref[h] = jnp.broadcast_to(total, (256, 128))
                o_ref[h] = part
            else:
                alpha = jnp.exp(old - new)
                l_ref[h] = l_ref[h] * alpha + total
                o_ref[h] = o_ref[h] * alpha + part
            m_ref[h] = new

    def attend(r):
        todo = []
        if 1 <= r <= 3:
            b = KV.block(r)
            KV.sib_wait(x, r)
            todo.append((x, b, b < zlo))
        if 1 <= r <= 4:
            KV.sib_wait(xm, r - 1)
            KV.sib_wait(xp, r - 1)
            todo.append((x - 1, KV.block(r - 1), x >= 1))
        if 2 <= r <= 5:
            b = KV.block(r - 2)
            KV.sib_wait(xo, r - 2)
            todo.append((x - 2, b, (x >= 2) & (b >= zlo)))

        @pl.loop(0, len(todo))
        def _(i):
            x_, b, cond = todo[-1]
            for j in range(len(todo) - 1):
                x_ = jnp.where(i == j, todo[j][0], x_)
                b = jnp.where(i == j, todo[j][1], b)
                cond = ((i == j) & todo[j][2]) | ((i != j) & cond)

            @pl.when(cond)
            def _():
                chunk(x_, b, False)

    KV.sib_wait(x, 0)
    chunk(x, zlo, True)
    for r in range(4):
        KV.x_fwd(r)
        if r < 3:
            KV.z_step(r + 1, 0)
            KV.z_step(r + 1, 1)
        KV.x_rest(r)
        if r > 0:
            KV.opp_step(r - 1)
        if r > 0:
            attend(r)
    KV.opp_step(3)
    attend(4)
    attend(5)

    for h in range(4):
        att_out[:, h * 128 : (h + 1) * 128] = (o_ref[h] / l_ref[h]).astype(jnp.bfloat16)
        logs = m_ref[h] + jnp.log(l_ref[h])
        for i in (0, 1):
            lse_out[h : h + 1, i * 128 : (i + 1) * 128] = jnp.transpose(
                logs[i * 128 : (i + 1) * 128, :]
            )[0:1, :]

    for cond, d in sent:
        if cond is None:
            d.wait_send()
        else:
            @pl.when(cond)
            def _(d=d):
                d.wait_send()


def on_device(hidden, gain, w_query, w_key, w_value, doc_ids):
    bf, f32 = jnp.bfloat16, jnp.float32
    hid = hidden.reshape(2, 128, 1024)
    tile = jnp.concatenate([doc_ids.reshape(2, 128), jnp.full((6, 128), 1 << 20, jnp.int32)], axis=0)
    gains = gain.astype(f32).reshape(8, 128)
    freq = np.exp(np.arange(64, dtype=np.float32) * np.float32(-2.0 * log_theta / 128))
    freq = jnp.asarray(np.tile(np.concatenate([freq, freq])[None], (8, 1)).astype(np.float32))
    dma = pltpu.SemaphoreType.DMA
    any_, vm = pl.BlockSpec(memory_space=pl.ANY), pl.BlockSpec(memory_space=pltpu.VMEM)
    mixed, cache, sums = pl.pallas_call(
        fused,
        out_shape=(
            jax.ShapeDtypeStruct((256, 512), bf),
            jax.ShapeDtypeStruct((2, 256, 128), bf),
            jax.ShapeDtypeStruct((4, 256), f32),
        ),
        in_specs=[any_] * 6 + [vm],
        out_specs=(vm, vm, vm),
        scratch_shapes=[
            pltpu.VMEM((8, 2, 128, 1024), bf),
            pltpu.VMEM((2, 128, 1024), bf),
            pltpu.VMEM((32, 256, 256), bf),
            pltpu.VMEM((2, 4, 4, 2, 128, 768), bf),
            pltpu.VMEM((2, 4, 4, 2, 256, 128), bf),
            pltpu.VMEM((2, 4, 4, 8, 128), jnp.int32),
            pltpu.VMEM((4, 2, 8, 128), f32),
            pltpu.VMEM((256, 768), f32),
            pltpu.VMEM((4, 256, 128), bf),
            pltpu.VMEM((256, 128), f32),
            pltpu.VMEM((256, 128), f32),
            pltpu.VMEM((256, 128), f32),
            pltpu.VMEM((4, 256, 128), f32),
            pltpu.VMEM((4, 256, 128), f32),
            pltpu.VMEM((4, 256, 128), f32),
            dma((6,)), dma((11,)), dma((11,)), dma((2, 2, 2)), dma((2, 2, 2)),
            dma((2, 2, 2)), dma((2, 2, 2)), dma((2, 2)), dma((2, 2)),
        ]
        + [
            dma((2, 4, 2)), dma((4, 2)), dma((2, 4, 2)), dma((2, 4, 2)),
            dma((2, 4)), dma((2, 4)), dma((4, 4)), dma((4, 4)),
        ] * 2,
        compiler_params=pltpu.CompilerParams(
            collective_id=0, has_side_effects=True, vmem_limit_bytes=62 * 1024 * 1024
        ),
        name="fused",
    )(
        hid, gains, w_query.reshape(2, 128, 512), w_key.reshape(2, 128, 128),
        w_value.reshape(2, 128, 128), tile, freq,
    )
    return mixed, cache, sums


def solution(mesh):
    in_specs = (P("seq", "kv"), P("kv"), P("seq", "kv"), P("seq", "kv"), P("seq", "kv"), P("seq"))
    out_specs = (P("seq", "kv"), P(None, "seq", "kv"), P("kv", "seq"))
    return jax.shard_map(
        on_device, mesh=mesh, in_specs=in_specs, out_specs=out_specs, check_vma=False
    )
```

```python
import functools

import jax
import jax.numpy as jnp
import numpy as np
from jax import lax
from jax.experimental import pallas as pl
from jax.experimental.pallas import tpu as pltpu
from jax.sharding import PartitionSpec as P

eps = 1e-05
log_theta = 13.122363377404328
MESH = pl.DeviceIdType.MESH
NX, NZ, NY, NH = 4, 4, 4, 2
DOCS = 17


def fused(
    hid_in, gain_in, wq_in, wk_in, wv_in, ids_in, freq_in,
    att_out, cache_out, lse_out,
    hbuf, rbuf, nbuf, abuf, bbuf, kvbuf, ibuf, gbuf, acc_a, acc_b, qbuf, cosb, sinb, startb, m_ref, l_ref, o_ref,
    loc_sem, small_s, small_r, hz_s, hz_r, hy_s, hy_r, hf_s, hf_r,
    az_s, az_r, ax_s, ax_r, af_s, af_r, ac_s, ac_r,
    bz_s, bz_r, bx_s, bx_r, bf_s, bf_r, bc_s, bc_r,
    kz_s, kz_r, kx_s, kx_r, kf_s, kf_r, kc_s, kc_r,
):
    kv = lax.axis_index("kv")
    seq = lax.axis_index("seq")
    y, zhi = kv // 2, kv % 2
    c = seq % 2
    zlo = (seq // 2) % 4
    x = seq // 8
    zz = zhi * 4 + zlo

    def at(x_=None, y_=None, zlo_=None, zhi_=None, c_=None):
        x_ = x if x_ is None else x_
        y_ = y if y_ is None else y_
        zlo_ = zlo if zlo_ is None else zlo_
        zhi_ = zhi if zhi_ is None else zhi_
        c_ = c if c_ is None else c_
        return (y_ * 2 + zhi_, (x_ * 4 + zlo_) * 2 + c_)

    def ring_z(step):
        z_ = (zz + 8 + step) % 8
        return z_ % 4, z_ // 4

    xp, xm, xo = (x + 1) % 4, (x + 3) % 4, (x + 2) % 4
    yp, ym, yo = (y + 1) % 4, (y + 3) % 4, (y + 2) % 4
    up_lo, up_hi = ring_z(2)
    dn_lo, dn_hi = ring_z(-2)
    sib = at(c_=1 - c)
    dev_xp, dev_xm = at(x_=xp), at(x_=xm)
    dev_yp, dev_ym = at(y_=yp), at(y_=ym)
    dev_up2, dev_dn2 = at(zlo_=up_lo, zhi_=up_hi), at(zlo_=dn_lo, zhi_=dn_hi)
    dev_zu, dev_zd = at(zlo_=(zlo + 1) % 4), at(zlo_=(zlo + 3) % 4)
    dev_pair = at(zhi_=1 - zhi)

    def rc(src, dst, ss, rs, dev):
        return pltpu.make_async_remote_copy(
            src_ref=src, dst_ref=dst, send_sem=ss, recv_sem=rs, device_id=dev, device_id_type=MESH
        )

    sent = []

    def send(src, dst, ss, rs, dev):
        d = rc(src, dst, ss, rs, dev)
        d.start()
        sent.append((None, d))

    def send_if(cond, src, dst, ss, rs, dev):
        d = rc(src, dst, ss, rs, dev)

        @pl.when(cond)
        def _():
            d.start()

        sent.append((cond, d))

    def got(ref, ss, rs):
        rc(ref, ref, ss, rs, sib).wait_recv()

    amine = abuf.at[c, x, zlo]
    hmine = hbuf.at[kv]
    locals_ = [
        pltpu.make_async_copy(wq_in, bbuf.at[c, x, zlo], loc_sem.at[0]),
        pltpu.make_async_copy(wk_in, amine.at[:, :, pl.ds(0, 128)], loc_sem.at[1]),
        pltpu.make_async_copy(wv_in, amine.at[:, :, pl.ds(128, 128)], loc_sem.at[2]),
        pltpu.make_async_copy(hid_in, hmine, loc_sem.at[3]),
        pltpu.make_async_copy(ids_in, ibuf.at[c, x, zlo], loc_sem.at[4]),
        pltpu.make_async_copy(gain_in, gbuf.at[y, zhi], loc_sem.at[5]),
    ]
    for d in locals_:
        d.start()

    barrier = pltpu.get_barrier_semaphore()
    peers = [sib, dev_pair, dev_up2, dev_dn2]
    for d in (1, 2, 3):
        peers += [at(x_=(x + d) % 4), at(y_=(y + d) % 4), at(zlo_=(zlo + d) % 4)]
    for dev in peers:
        pl.semaphore_signal(barrier, inc=1, device_id=dev, device_id_type=MESH)
    for d in locals_:
        d.wait()
    pl.semaphore_wait(barrier, len(peers))

    for d in (1, 2, 3):
        t = ibuf.at[c, x, zlo]
        send(t, t, small_s.at[d - 1], small_r.at[d - 1], at(zlo_=(zlo + d) % 4))
    t = gbuf.at[y, zhi]
    send(t, t, small_s.at[3], small_r.at[3], dev_pair)

    class Gather:
        def __init__(self, buf, zs, zr, xs, xr, fs, fr, cs, cr):
            self.buf, self.zs, self.zr, self.xs, self.xr = buf, zs, zr, xs, xr
            self.fs, self.fr, self.cs, self.cr = fs, fr, cs, cr

        def block(self, r):
            if r == 0:
                return zlo
            mid = {1: (0, 3), 2: (2, 1), 3: (3, 0)}[r]
            return jnp.where(
                zlo == 0, r, jnp.where(zlo == 3, 3 - r, jnp.where(zlo == 1, mid[0], mid[1]))
            )

        def to_sib(self, x_, b):
            s = self.buf.at[c, x_, b]
            send(s, s, self.cs.at[x_, b], self.cr.at[x_, b], sib)

        def z_part(self, b, h):
            s = self.buf.at[c, x, b, h]
            send_if((zlo < 3) & (b <= zlo), s, s, self.zs.at[0, b, h], self.zr.at[b, h], dev_zu)
            send_if((zlo > 0) & (b >= zlo), s, s, self.zs.at[1, b, h], self.zr.at[b, h], dev_zd)

        def x_part(self, b, h, way):
            s = self.buf.at[c, x, b, h]
            send(s, s, self.xs.at[way, b, h], self.xr.at[way, b, h], (dev_xp, dev_xm)[way])

        def z_first(self):
            for h in (0, 1):
                self.z_part(zlo, h)

        def x_first(self):
            for h in (0, 1):
                self.x_part(zlo, h, 0)
                self.x_part(zlo, 1 - h, 1)
            self.to_sib(x, zlo)

        def z_step(self, r, h):
            b = self.block(r)
            got(self.buf.at[c, x, b, h], self.zs.at[0, b, h], self.zr.at[b, h])
            self.z_part(b, h)
            self.x_part(b, h, 0)
            self.x_part(b, h, 1)
            if h == 1:
                self.to_sib(x, b)

        def x_fwd(self, r):
            b = self.block(r)
            t = self.buf.at[c, xm, b, 0]
            got(t, self.xs.at[0, b, 0], self.xr.at[0, b, 0])
            send(t, t, self.fs.at[0, b], self.fr.at[0, b], dev_xp)
            t = self.buf.at[c, xp, b, 1]
            got(t, self.xs.at[1, b, 1], self.xr.at[1, b, 1])
            send(t, t, self.fs.at[1, b], self.fr.at[1, b], dev_xm)

        def x_rest(self, r):
            b = self.block(r)
            got(self.buf.at[c, xm, b, 1], self.xs.at[0, b, 1], self.xr.at[0, b, 1])
            self.to_sib(xm, b)
            got(self.buf.at[c, xp, b, 0], self.xs.at[1, b, 0], self.xr.at[1, b, 0])
            self.to_sib(xp, b)

        def opp_step(self, r):
            b = self.block(r)
            t = self.buf.at[c, xo, b]
            got(t.at[0], self.fs.at[0, b], self.fr.at[0, b])
            got(t.at[1], self.fs.at[1, b], self.fr.at[1, b])
            self.to_sib(xo, b)

        def sib_wait(self, x_, r):
            b = self.block(r)
            got(self.buf.at[1 - c, x_, b], self.cs.at[x_, b], self.cr.at[x_, b])

    A = Gather(abuf, az_s, az_r, ax_s, ax_r, af_s, af_r, ac_s, ac_r)
    B = Gather(bbuf, bz_s, bz_r, bx_s, bx_r, bf_s, bf_r, bc_s, bc_r)
    KV = Gather(kvbuf, kz_s, kz_r, kx_s, kx_r, kf_s, kf_r, kc_s, kc_r)

    def y_part(g, zh, h, way, rows):
        t = hbuf.at[y * 2 + zh, h, rows]
        send(t, t, hy_s.at[g, way, h], hy_r.at[g, way, h], (dev_yp, dev_ym)[way])

    def y_fwd(g, zh, rows):
        t = hbuf.at[ym * 2 + zh, 0, rows]
        got(t, hy_s.at[g, 0, 0], hy_r.at[g, 0, 0])
        send(t, t, hf_s.at[g, 0], hf_r.at[g, 0], dev_yp)
        t = hbuf.at[yp * 2 + zh, 1, rows]
        got(t, hy_s.at[g, 1, 1], hy_r.at[g, 1, 1])
        send(t, t, hf_s.at[g, 1], hf_r.at[g, 1], dev_ym)

    def y_end(g, zh, rows):
        got(hbuf.at[ym * 2 + zh, 1, rows], hy_s.at[g, 0, 1], hy_r.at[g, 0, 1])
        got(hbuf.at[yp * 2 + zh, 0, rows], hy_s.at[g, 1, 0], hy_r.at[g, 1, 0])
        for h in (0, 1):
            got(hbuf.at[yo * 2 + zh, h, rows], hf_s.at[g, h], hf_r.at[g, h])

    everyrow = pl.ds(0, 128)
    quarter = [pl.ds(0, 64), pl.ds(64, 64)]

    def relay(p):
        for way, hi, dev in ((0, dn_hi, dev_up2), (1, up_hi, dev_dn2)):
            t = rbuf.at[way, quarter[p]]
            got(t, hz_s.at[0, way, p], hz_r.at[0, way, p])
            send(
                t, hbuf.at[y * 2 + hi, way, quarter[p]],
                hz_s.at[1, way, p], hz_r.at[1, way, p], dev,
            )

    def cross(p):
        for h in (0, 1):
            t = hbuf.at[y * 2 + 1 - zhi, h, quarter[p]]
            got(t, hz_s.at[1, h, p], hz_r.at[1, h, p])
            y_part(1 + p, 1 - zhi, h, 0, quarter[p])
            y_part(1 + p, 1 - zhi, h, 1, quarter[p])

    def hz_send(p):
        for way, dev in ((0, dev_up2), (1, dev_dn2)):
            send(
                hmine.at[way, quarter[p]], rbuf.at[way, quarter[p]],
                hz_s.at[0, way, p], hz_r.at[0, way, p], dev,
            )

    def hy_send():
        for h in (0, 1):
            y_part(0, zhi, h, 0, everyrow)
            y_part(0, zhi, 1 - h, 1, everyrow)

    def small_two():
        for d in (1, 2, 3):
            got(ibuf.at[c, x, (zlo + 4 - d) % 4], small_s.at[d - 1], small_r.at[d - 1])
        got(gbuf.at[y, 1 - zhi], small_s.at[3], small_r.at[3])
        for d in (1, 2, 3):
            t = ibuf.at[c, x]
            send(t, t, small_s.at[3 + d], small_r.at[3 + d], at(x_=(x + d) % 4))
            t = gbuf.at[y]
            send(t, t, small_s.at[6 + d], small_r.at[6 + d], at(y_=(y + d) % 4))

    def small_three():
        for d in (1, 2, 3):
            got(ibuf.at[c, (x + 4 - d) % 4], small_s.at[3 + d], small_r.at[3 + d])
            got(gbuf.at[(y + 4 - d) % 4], small_s.at[6 + d], small_r.at[6 + d])
        t = ibuf.at[c]
        send(t, t, small_s.at[10], small_r.at[10], sib)

    def squares(zh, total):
        def one(i, total):
            for j in range(8):
                h = hbuf[i * 2 + zh, :, :, j * 128 : (j + 1) * 128].reshape(256, 128)
                h = h.astype(jnp.float32)
                total = total + h * h
            return total

        return lax.fori_loop(0, 4, one, total)

    def multiply(G, acc, nbuf_, r, width):
        b = G.block(r)

        @pl.loop(0, 8)
        def _(i):
            x_, c_ = i // 2, i % 2
            w = G.buf[c_, x_, b].reshape(256, width)
            acc[...] += jnp.dot(
                nbuf_[(x_ * 4 + b) * 2 + c_], w, preferred_element_type=jnp.float32
            )

    def sib_all(G, r):
        for x_ in (x, xm, xp, xo):
            G.sib_wait(x_, r)

    def turn(u):
        return u * cosb[...] + pltpu.roll(u, 64, 1) * sinb[...]

    def tables():
        got(ibuf.at[1 - c], small_s.at[10], small_r.at[10])
        every = ibuf[...].reshape(32, 2, 128)
        mine = ibuf[c, x, zlo].astype(jnp.float32)
        idc = jnp.concatenate(
            [jnp.transpose(jnp.broadcast_to(mine[i : i + 1, :], (128, 128))) for i in (0, 1)], axis=0
        )
        start = jnp.zeros((256, 128), jnp.float32)
        for d in range(DOCS - 1):
            hits = jnp.sum(jnp.where(every == d, 1.0, 0.0), axis=0)
            held = jnp.sum(jnp.sum(hits, axis=0, keepdims=True), axis=1, keepdims=True)
            start = start + jnp.where(idc > d, held, 0.0)
        startb[...] = start
        row = lax.broadcasted_iota(jnp.int32, (256, 128), 0).astype(jnp.float32)
        tok = row + (seq * 256).astype(jnp.float32)
        angle = (tok - start) * freq_in[0:1, :]
        lane = lax.broadcasted_iota(jnp.int32, (256, 128), 1)
        cosb[...] = jnp.cos(angle)
        sinb[...] = jnp.where(lane < 64, -1.0, 1.0) * jnp.sin(angle)

    def normalise(total):
        total = squares(1 - zhi, total)
        factor = lax.rsqrt(jnp.sum(total, axis=1, keepdims=True) * (1.0 / 8192.0) + eps)
        factor = jnp.broadcast_to(factor, (256, 128))

        @pl.loop(0, 8)
        def _(k):
            g = gbuf[k // 2, k % 2].astype(jnp.float32)
            for i in range(8):
                h = hbuf[k, :, :, i * 128 : (i + 1) * 128].reshape(256, 128).astype(jnp.float32)
                nbuf[k * 4 + i // 2, :, (i % 2) * 128 : (i % 2 + 1) * 128] = (
                    h * factor * g[i : i + 1, :]
                ).astype(jnp.bfloat16)

    def keys_values():
        kmine = turn(acc_a[:, 0:128]).astype(jnp.bfloat16)
        vmine = acc_a[:, 128:256].astype(jnp.bfloat16)
        kvbuf[c, x, zlo, 0] = kmine
        kvbuf[c, x, zlo, 1] = vmine
        cache_out[0] = kmine
        cache_out[1] = vmine

    def queries():
        for h in range(4):
            qbuf[h] = turn(acc_b[:, h * 128 : (h + 1) * 128]).astype(jnp.bfloat16)

    scale = 128 ** (-0.5)
    lane_f = lax.broadcasted_iota(jnp.int32, (1, 512), 1).astype(jnp.float32)

    def chunk(x_, b, first):
        base = ((x_ * 4 + b) * 512).astype(jnp.float32)
        keys = kvbuf[:, x_, b, 0].reshape(512, 128)
        vals = kvbuf[:, x_, b, 1].reshape(512, 128)
        low = startb[:, 0:1] - base
        seen = lane_f >= low
        if first:
            here = (
                lax.broadcasted_iota(jnp.int32, (256, 1), 0).astype(jnp.float32)
                + (c * 256).astype(jnp.float32)
            )
            seen = seen & (lane_f <= here)
        for h in range(4):
            s = lax.dot_general(
                qbuf[h], keys, (((1,), (1,)), ((), ())), preferred_element_type=jnp.float32
            )
            s = jnp.where(seen, s * scale, -1e30)
            top = jnp.max(s, axis=1, keepdims=True)
            if first:
                new = jnp.broadcast_to(top, (256, 128))
            else:
                old = m_ref[h]
                new = jnp.maximum(old, top)
            p = jnp.exp(s - new[:, 0:1])
            total = jnp.sum(p, axis=1, keepdims=True)
            part = jnp.dot(p.astype(jnp.bfloat16), vals, preferred_element_type=jnp.float32)
            if first:
                l_ref[h] = jnp.broadcast_to(total, (256, 128))
                o_ref[h] = part
            else:
                alpha = jnp.exp(old - new)
                l_ref[h] = l_ref[h] * alpha + total
                o_ref[h] = o_ref[h] * alpha + part
            m_ref[h] = new

    def attend(r):
        if r == 0:
            KV.sib_wait(x, 0)
            chunk(x, zlo, True)
            return
        todo = []
        if 1 <= r <= 3:
            b = KV.block(r)
            KV.sib_wait(x, r)
            todo.append((x, b, b < zlo))
        if 1 <= r <= 4:
            KV.sib_wait(xm, r - 1)
            KV.sib_wait(xp, r - 1)
            todo.append((x - 1, KV.block(r - 1), x >= 1))
        if 2 <= r <= 5:
            b = KV.block(r - 2)
            KV.sib_wait(xo, r - 2)
            todo.append((x - 2, b, (x >= 2) & (b >= zlo)))

        @pl.loop(0, len(todo))
        def _(i):
            x_, b, cond = todo[-1]
            for j in range(len(todo) - 1):
                x_ = jnp.where(i == j, todo[j][0], x_)
                b = jnp.where(i == j, todo[j][1], b)
                cond = ((i == j) & todo[j][2]) | ((i != j) & cond)

            @pl.when(cond)
            def _():
                chunk(x_, b, False)

    def finish():
        for h in range(4):
            att_out[:, h * 128 : (h + 1) * 128] = (o_ref[h] / l_ref[h]).astype(jnp.bfloat16)
            logs = m_ref[h] + jnp.log(l_ref[h])
            for i in (0, 1):
                lse_out[h : h + 1, i * 128 : (i + 1) * 128] = jnp.transpose(
                    logs[i * 128 : (i + 1) * 128, :]
                )[0:1, :]

    acc_a[...] = jnp.zeros_like(acc_a)
    acc_b[...] = jnp.zeros_like(acc_b)

    A.z_first()
    B.x_first()
    hz_send(0)
    B.z_first()
    B.x_fwd(0)
    hz_send(1)
    A.z_step(1, 0)
    A.x_first()
    hy_send()
    A.z_step(1, 1)
    A.x_fwd(0)
    small_two()
    A.opp_step(0)
    y_fwd(0, zhi, everyrow)
    A.x_fwd(1)
    A.z_step(2, 0)
    relay(0)
    A.z_step(2, 1)
    B.z_step(1, 0)
    relay(1)
    B.z_step(1, 1)
    A.x_rest(1)
    cross(0)
    small_three()
    A.x_fwd(2)
    A.z_step(3, 0)
    A.z_step(3, 1)
    B.x_fwd(1)
    cross(1)
    y_fwd(1, 1 - zhi, quarter[0])
    B.z_step(3, 0)
    y_end(0, zhi, everyrow)
    A.x_fwd(3)
    B.x_rest(1)
    A.x_rest(3)
    B.z_step(2, 0)
    A.opp_step(1)
    y_fwd(2, 1 - zhi, quarter[1])
    A.x_rest(0)
    A.opp_step(2)
    A.opp_step(3)
    B.z_step(3, 1)
    total = squares(zhi, jnp.zeros((256, 128), jnp.float32))
    tables()
    B.z_step(2, 1)
    B.x_fwd(3)
    y_end(1, 1 - zhi, quarter[0])
    y_end(2, 1 - zhi, quarter[1])
    A.x_rest(2)
    normalise(total)
    sib_all(A, 1)
    multiply(A, acc_a, nbuf, 1, 256)
    B.x_fwd(2)
    B.x_rest(2)
    B.x_rest(0)
    B.x_rest(3)
    sib_all(A, 2)
    multiply(A, acc_a, nbuf, 2, 256)
    sib_all(A, 3)
    multiply(A, acc_a, nbuf, 3, 256)
    sib_all(A, 0)
    multiply(A, acc_a, nbuf, 0, 256)
    keys_values()
    B.opp_step(3)
    KV.z_first()
    KV.x_first()
    B.opp_step(2)
    KV.z_step(2, 0)
    B.opp_step(1)
    sib_all(B, 1)
    multiply(B, acc_b, nbuf, 1, 512)
    B.opp_step(0)
    KV.z_step(1, 0)
    KV.x_fwd(0)
    KV.z_step(2, 1)
    sib_all(B, 3)
    multiply(B, acc_b, nbuf, 3, 512)
    sib_all(B, 2)
    multiply(B, acc_b, nbuf, 2, 512)
    sib_all(B, 0)
    multiply(B, acc_b, nbuf, 0, 512)
    queries()
    KV.z_step(1, 1)
    attend(0)
    KV.x_rest(0)
    KV.z_step(3, 0)
    KV.opp_step(0)
    KV.z_step(3, 1)
    KV.x_fwd(1)
    KV.x_rest(1)
    KV.x_fwd(2)
    KV.x_rest(2)
    attend(1)
    attend(2)
    KV.opp_step(1)
    KV.x_fwd(3)
    KV.x_rest(3)
    KV.opp_step(2)
    attend(3)
    KV.opp_step(3)
    attend(4)
    attend(5)
    finish()

    for cond, d in sent:
        if cond is None:
            d.wait_send()
        else:
            @pl.when(cond)
            def _(d=d):
                d.wait_send()


def on_device(hidden, gain, w_query, w_key, w_value, doc_ids):
    bf, f32 = jnp.bfloat16, jnp.float32
    hid = hidden.reshape(2, 128, 1024)
    tile = doc_ids.reshape(2, 128)
    gains = gain.reshape(8, 128)
    freq = np.exp(np.arange(64, dtype=np.float32) * np.float32(-2.0 * log_theta / 128))
    freq = jnp.asarray(np.tile(np.concatenate([freq, freq])[None], (8, 1)).astype(np.float32))
    dma = pltpu.SemaphoreType.DMA
    any_, vm = pl.BlockSpec(memory_space=pl.ANY), pl.BlockSpec(memory_space=pltpu.VMEM)
    mixed, cache, sums = pl.pallas_call(
        fused,
        out_shape=(
            jax.ShapeDtypeStruct((256, 512), bf),
            jax.ShapeDtypeStruct((2, 256, 128), bf),
            jax.ShapeDtypeStruct((4, 256), f32),
        ),
        in_specs=[any_] * 6 + [vm],
        out_specs=(vm, vm, vm),
        scratch_shapes=[
            pltpu.VMEM((8, 2, 128, 1024), bf),
            pltpu.VMEM((2, 128, 1024), bf),
            pltpu.VMEM((32, 256, 256), bf),
            pltpu.VMEM((2, 4, 4, 2, 128, 256), bf),
            pltpu.VMEM((2, 4, 4, 2, 128, 512), bf),
            pltpu.VMEM((2, 4, 4, 2, 256, 128), bf),
            pltpu.VMEM((2, 4, 4, 2, 128), jnp.int32),
            pltpu.VMEM((4, 2, 8, 128), bf),
            pltpu.VMEM((256, 256), f32),
            pltpu.VMEM((256, 512), f32),
            pltpu.VMEM((4, 256, 128), bf),
            pltpu.VMEM((256, 128), f32),
            pltpu.VMEM((256, 128), f32),
            pltpu.VMEM((256, 128), f32),
            pltpu.VMEM((4, 256, 128), f32),
            pltpu.VMEM((4, 256, 128), f32),
            pltpu.VMEM((4, 256, 128), f32),
            dma((6,)), dma((11,)), dma((11,)), dma((2, 2, 2)), dma((2, 2, 2)),
            dma((3, 2, 2)), dma((3, 2, 2)), dma((3, 2)), dma((3, 2)),
        ]
        + [
            dma((2, 4, 2)), dma((4, 2)), dma((2, 4, 2)), dma((2, 4, 2)),
            dma((2, 4)), dma((2, 4)), dma((4, 4)), dma((4, 4)),
        ] * 3,
        compiler_params=pltpu.CompilerParams(
            collective_id=0, has_side_effects=True, vmem_limit_bytes=62 * 1024 * 1024
        ),
        name="fused",
    )(
        hid, gains, w_query.reshape(2, 128, 512), w_key.reshape(2, 128, 128),
        w_value.reshape(2, 128, 128), tile, freq,
    )
    return mixed, cache, sums


def solution(mesh):
    in_specs = (P("seq", "kv"), P("kv"), P("seq", "kv"), P("seq", "kv"), P("seq", "kv"), P("seq"))
    out_specs = (P("seq", "kv"), P(None, "seq", "kv"), P("kv", "seq"))
    return jax.shard_map(
        on_device, mesh=mesh, in_specs=in_specs, out_specs=out_specs, check_vma=False
    )
```

```python
import functools

import jax
import jax.numpy as jnp
import numpy as np
from jax import lax
from jax.experimental import pallas as pl
from jax.experimental.pallas import tpu as pltpu
from jax.sharding import PartitionSpec as P

eps = 1e-05
log_theta = 13.122363377404328
MESH = pl.DeviceIdType.MESH
NX, NZ, NY, NH = 4, 4, 4, 2
DOCS = 17


def fused(
    hid_in, gain_in, wq_in, wk_in, wv_in, ids_in, freq_in,
    att_out, cache_out, lse_out,
    hbuf, rbuf, nbuf, abuf, bbuf, kvbuf, ibuf, gbuf, acc_b, qbuf, cosb, sinb, startr, m_ref, l_ref, o_ref,
    loc_sem, small_s, small_r, hz_s, hz_r, hy_s, hy_r, hf_s, hf_r,
    az_s, az_r, ax_s, ax_r, af_s, af_r, ac_s, ac_r,
    bz_s, bz_r, bx_s, bx_r, bf_s, bf_r, bc_s, bc_r,
    kz_s, kz_r, kx_s, kx_r, kf_s, kf_r, kc_s, kc_r,
):
    kv = lax.axis_index("kv")
    seq = lax.axis_index("seq")
    y, zhi = kv // 2, kv % 2
    c = seq % 2
    zlo = (seq // 2) % 4
    x = seq // 8
    zz = zhi * 4 + zlo

    def at(x_=None, y_=None, zlo_=None, zhi_=None, c_=None):
        x_ = x if x_ is None else x_
        y_ = y if y_ is None else y_
        zlo_ = zlo if zlo_ is None else zlo_
        zhi_ = zhi if zhi_ is None else zhi_
        c_ = c if c_ is None else c_
        return (y_ * 2 + zhi_, (x_ * 4 + zlo_) * 2 + c_)

    def ring_z(step):
        z_ = (zz + 8 + step) % 8
        return z_ % 4, z_ // 4

    xp, xm, xo = (x + 1) % 4, (x + 3) % 4, (x + 2) % 4
    yp, ym, yo = (y + 1) % 4, (y + 3) % 4, (y + 2) % 4
    up_lo, up_hi = ring_z(2)
    dn_lo, dn_hi = ring_z(-2)
    sib = at(c_=1 - c)
    dev_xp, dev_xm = at(x_=xp), at(x_=xm)
    dev_yp, dev_ym = at(y_=yp), at(y_=ym)
    dev_up2, dev_dn2 = at(zlo_=up_lo, zhi_=up_hi), at(zlo_=dn_lo, zhi_=dn_hi)
    dev_zu, dev_zd = at(zlo_=(zlo + 1) % 4), at(zlo_=(zlo + 3) % 4)
    dev_pair = at(zhi_=1 - zhi)

    def rc(src, dst, ss, rs, dev):
        return pltpu.make_async_remote_copy(
            src_ref=src, dst_ref=dst, send_sem=ss, recv_sem=rs, device_id=dev, device_id_type=MESH
        )

    sent = []

    def send(src, dst, ss, rs, dev):
        d = rc(src, dst, ss, rs, dev)
        d.start()
        sent.append((None, d))

    def send_if(cond, src, dst, ss, rs, dev):
        d = rc(src, dst, ss, rs, dev)

        @pl.when(cond)
        def _():
            d.start()

        sent.append((cond, d))

    def got(ref, ss, rs):
        rc(ref, ref, ss, rs, sib).wait_recv()

    amine = abuf.at[c, x, zlo]
    hmine = hbuf.at[kv]
    locals_ = [
        pltpu.make_async_copy(wq_in, bbuf.at[c, x, zlo], loc_sem.at[0]),
        pltpu.make_async_copy(wk_in, amine.at[:, :, pl.ds(0, 128)], loc_sem.at[1]),
        pltpu.make_async_copy(wv_in, amine.at[:, :, pl.ds(128, 128)], loc_sem.at[2]),
        pltpu.make_async_copy(hid_in, hmine, loc_sem.at[3]),
        pltpu.make_async_copy(ids_in, ibuf.at[c, x, zlo], loc_sem.at[4]),
        pltpu.make_async_copy(gain_in, gbuf.at[y, zhi], loc_sem.at[5]),
    ]
    for d in locals_:
        d.start()

    barrier = pltpu.get_barrier_semaphore()
    peers = [sib, dev_pair, dev_up2, dev_dn2]
    for d in (1, 2, 3):
        peers += [at(x_=(x + d) % 4), at(y_=(y + d) % 4), at(zlo_=(zlo + d) % 4)]
    for dev in peers:
        pl.semaphore_signal(barrier, inc=1, device_id=dev, device_id_type=MESH)
    for d in locals_:
        d.wait()
    pl.semaphore_wait(barrier, len(peers))

    for d in (1, 2, 3):
        t = ibuf.at[c, x, zlo]
        send(t, t, small_s.at[d - 1], small_r.at[d - 1], at(zlo_=(zlo + d) % 4))
    t = gbuf.at[y, zhi]
    send(t, t, small_s.at[3], small_r.at[3], dev_pair)

    class Gather:
        def __init__(self, buf, zs, zr, xs, xr, fs, fr, cs, cr, back_only=False):
            self.back_only = back_only
            self.buf, self.zs, self.zr, self.xs, self.xr = buf, zs, zr, xs, xr
            self.fs, self.fr, self.cs, self.cr = fs, fr, cs, cr

        def block(self, r):
            if r == 0:
                return zlo
            mid = {1: (0, 3), 2: (2, 1), 3: (3, 0)}[r]
            return jnp.where(
                zlo == 0, r, jnp.where(zlo == 3, 3 - r, jnp.where(zlo == 1, mid[0], mid[1]))
            )

        def to_sib(self, x_, b, h):
            s = self.buf.at[c, x_, b, h]
            send(s, s, self.cs.at[x_, b, h], self.cr.at[x_, b, h], sib)

        def z_part(self, b, h):
            s = self.buf.at[c, x, b, h]
            send_if((zlo < 3) & (b <= zlo), s, s, self.zs.at[0, b, h], self.zr.at[b, h], dev_zu)
            send_if((zlo > 0) & (b >= zlo), s, s, self.zs.at[1, b, h], self.zr.at[b, h], dev_zd)

        def x_part(self, b, h):
            s = self.buf.at[c, x, b, h]
            send(s, s, self.xs.at[0, b, h], self.xr.at[0, b, h], dev_xp)
            if h == 1 or not self.back_only:
                send(s, s, self.xs.at[1, b, h], self.xr.at[1, b, h], dev_xm)
            self.to_sib(x, b, h)

        def z_first(self, h):
            self.z_part(zlo, h)

        def x_first(self, h):
            self.x_part(zlo, h)

        def z_step(self, r, h):
            b = self.block(r)
            got(self.buf.at[c, x, b, h], self.zs.at[0, b, h], self.zr.at[b, h])
            self.z_part(b, h)
            self.x_part(b, h)

        def x_fwd(self, r, h):
            b = self.block(r)
            x_, dev = ((xm, dev_xp), (xp, dev_xm))[h]
            t = self.buf.at[c, x_, b, h]
            got(t, self.xs.at[h, b, h], self.xr.at[h, b, h])
            send(t, t, self.fs.at[h, b], self.fr.at[h, b], dev)
            if h == 0 or not self.back_only:
                self.to_sib(x_, b, h)

        def x_rest(self, r):
            b = self.block(r)
            got(self.buf.at[c, xm, b, 1], self.xs.at[0, b, 1], self.xr.at[0, b, 1])
            self.to_sib(xm, b, 1)
            if not self.back_only:
                got(self.buf.at[c, xp, b, 0], self.xs.at[1, b, 0], self.xr.at[1, b, 0])
                self.to_sib(xp, b, 0)

        def opp_step(self, r, h):
            b = self.block(r)
            t = self.buf.at[c, xo, b, h]
            got(t, self.fs.at[h, b], self.fr.at[h, b])
            self.to_sib(xo, b, h)

        def sib_wait(self, x_, r):
            b = self.block(r)
            for h in (0, 1):
                got(self.buf.at[1 - c, x_, b, h], self.cs.at[x_, b, h], self.cr.at[x_, b, h])

    A = Gather(abuf, az_s, az_r, ax_s, ax_r, af_s, af_r, ac_s, ac_r)
    B = Gather(bbuf, bz_s, bz_r, bx_s, bx_r, bf_s, bf_r, bc_s, bc_r)
    KV = Gather(kvbuf, kz_s, kz_r, kx_s, kx_r, kf_s, kf_r, kc_s, kc_r, True)

    def y_part(g, zh, h, way, p):
        t = hbuf.at[y * 2 + zh, p, h]
        send(t, t, hy_s.at[g, way, h], hy_r.at[g, way, h], (dev_yp, dev_ym)[way])

    def y_fwd(g, zh, p):
        t = hbuf.at[ym * 2 + zh, p, 0]
        got(t, hy_s.at[g, 0, 0], hy_r.at[g, 0, 0])
        send(t, t, hf_s.at[g, 0], hf_r.at[g, 0], dev_yp)
        t = hbuf.at[yp * 2 + zh, p, 1]
        got(t, hy_s.at[g, 1, 1], hy_r.at[g, 1, 1])
        send(t, t, hf_s.at[g, 1], hf_r.at[g, 1], dev_ym)

    def y_end(g, zh, p):
        got(hbuf.at[ym * 2 + zh, p, 1], hy_s.at[g, 0, 1], hy_r.at[g, 0, 1])
        got(hbuf.at[yp * 2 + zh, p, 0], hy_s.at[g, 1, 0], hy_r.at[g, 1, 0])
        for h in (0, 1):
            got(hbuf.at[yo * 2 + zh, p, h], hf_s.at[g, h], hf_r.at[g, h])

    def hz_send(p):
        for way, dev in ((0, dev_up2), (1, dev_dn2)):
            send(
                hmine.at[p, way], rbuf.at[p, way],
                hz_s.at[0, way, p], hz_r.at[0, way, p], dev,
            )

    def relay(p):
        for way, hi, dev in ((0, dn_hi, dev_up2), (1, up_hi, dev_dn2)):
            t = rbuf.at[p, way]
            got(t, hz_s.at[0, way, p], hz_r.at[0, way, p])
            send(
                t, hbuf.at[y * 2 + hi, p, way],
                hz_s.at[1, way, p], hz_r.at[1, way, p], dev,
            )

    def cross(p):
        for h in (0, 1):
            t = hbuf.at[y * 2 + 1 - zhi, p, h]
            got(t, hz_s.at[1, h, p], hz_r.at[1, h, p])
            y_part(2 + p, 1 - zhi, h, 0, p)
            y_part(2 + p, 1 - zhi, h, 1, p)

    def hy_send(p):
        for h in (0, 1):
            y_part(p, zhi, h, 0, p)
            y_part(p, zhi, 1 - h, 1, p)

    def small_two():
        for d in (1, 2, 3):
            got(ibuf.at[c, x, (zlo + 4 - d) % 4], small_s.at[d - 1], small_r.at[d - 1])
        got(gbuf.at[y, 1 - zhi], small_s.at[3], small_r.at[3])
        for d in (1, 2, 3):
            t = ibuf.at[c, x]
            send(t, t, small_s.at[3 + d], small_r.at[3 + d], at(x_=(x + d) % 4))
            t = gbuf.at[y]
            send(t, t, small_s.at[6 + d], small_r.at[6 + d], at(y_=(y + d) % 4))

    def small_three():
        for d in (1, 2, 3):
            got(ibuf.at[c, (x + 4 - d) % 4], small_s.at[3 + d], small_r.at[3 + d])
            got(gbuf.at[(y + 4 - d) % 4], small_s.at[6 + d], small_r.at[6 + d])
        t = ibuf.at[c]
        send(t, t, small_s.at[10], small_r.at[10], sib)

    def squares(p, zh, total):
        def one(i, total):
            for j in range(8):
                h = hbuf[i * 2 + zh, p, :, :, j * 128 : (j + 1) * 128].reshape(128, 128)
                h = h.astype(jnp.float32)
                total = total + h * h
            return total

        return lax.fori_loop(0, 4, one, total)

    totals = [None, None]

    def own_squares():
        for p in (0, 1):
            totals[p] = squares(p, zhi, jnp.zeros((128, 128), jnp.float32))

    def multiply(G, acc, nbuf_, r, width):
        b = G.block(r)
        w = G.buf[:, :, b].reshape(2048, width)
        acc[...] += jnp.dot(nbuf_[b], w, preferred_element_type=jnp.float32)

    def sib_all(G, r):
        for x_ in (x, xm, xp, xo):
            G.sib_wait(x_, r)

    def turn(u, rows=slice(0, 256)):
        return u * cosb[rows, :] + pltpu.roll(u, 64, 1) * sinb[rows, :]

    def tables():
        got(ibuf.at[1 - c], small_s.at[10], small_r.at[10])
        every = ibuf[...].reshape(32, 2, 128)
        mine = ibuf[c, x, zlo].astype(jnp.float32)
        idc = jnp.concatenate(
            [jnp.transpose(jnp.broadcast_to(mine[i : i + 1, :], (128, 128))) for i in (0, 1)], axis=0
        )
        start = jnp.zeros((256, 128), jnp.float32)
        start_row = jnp.zeros((2, 128), jnp.float32)
        for d in range(DOCS - 1):
            hits = jnp.sum(jnp.where(every == d, 1.0, 0.0), axis=0)
            held = jnp.sum(jnp.sum(hits, axis=0, keepdims=True), axis=1, keepdims=True)
            start = start + jnp.where(idc > d, held, 0.0)
            start_row = start_row + jnp.where(mine > d, held, 0.0)
        for i in (0, 1):
            for h in range(4):
                startr[0:1, h * 256 + i * 128 : h * 256 + (i + 1) * 128] = start_row[i : i + 1, :]
        row = lax.broadcasted_iota(jnp.int32, (256, 128), 0).astype(jnp.float32)
        tok = row + (seq * 256).astype(jnp.float32)
        angle = (tok - start) * freq_in[0:1, :]
        lane = lax.broadcasted_iota(jnp.int32, (256, 128), 1)
        cosb[...] = jnp.cos(angle)
        sinb[...] = jnp.where(lane < 64, -1.0, 1.0) * jnp.sin(angle)

    def normalise(p):
        total = squares(p, 1 - zhi, totals[p])
        factor = lax.rsqrt(jnp.sum(total, axis=1, keepdims=True) * (1.0 / 8192.0) + eps)
        factor = jnp.broadcast_to(factor, (128, 128))

        @pl.loop(0, 8)
        def _(k):
            g = gbuf[k // 2, k % 2].astype(jnp.float32)
            for i in range(8):
                h = hbuf[k, p, :, :, i * 128 : (i + 1) * 128].reshape(128, 128)
                lane = pl.multiple_of(((i // 2) % 2 * 4 + k // 2) * 256 + (i % 2) * 128, 128)
                nbuf[(k % 2) * 2 + i // 4, p * 128 : (p + 1) * 128, pl.ds(lane, 128)] = (
                    h.astype(jnp.float32) * factor * g[i : i + 1, :]
                ).astype(jnp.bfloat16)

    def keys_values(p):
        rows = slice(p * 128, (p + 1) * 128)

        sums = jnp.zeros((128, 256), jnp.float32)
        for b in range(4):
            w = abuf[:, :, b].reshape(2048, 256)
            sums = sums + jnp.dot(nbuf[b, rows, :], w, preferred_element_type=jnp.float32)
        kmine = turn(sums[:, 0:128], rows).astype(jnp.bfloat16)
        vmine = sums[:, 128:256].astype(jnp.bfloat16)
        kvbuf[c, x, zlo, p, 0] = kmine
        kvbuf[c, x, zlo, p, 1] = vmine
        cache_out[0, rows, :] = kmine
        cache_out[1, rows, :] = vmine

    def queries():
        for h in range(4):
            q = turn(acc_b[:, h * 128 : (h + 1) * 128])
            qbuf[:, h * 256 : (h + 1) * 256] = jnp.transpose(q).astype(jnp.bfloat16)

    scale = 128 ** (-0.5)

    def chunk(x_, b, first):
        base = ((x_ * 4 + b) * 512).astype(jnp.float32)
        keys = kvbuf[:, x_, b, :, 0].reshape(512, 128)
        vals = jnp.transpose(kvbuf[:, x_, b, :, 1].reshape(512, 128))
        key = lax.broadcasted_iota(jnp.int32, (512, 1024), 0).astype(jnp.float32)
        seen = key >= startr[...] - base
        if first:
            here = lax.broadcasted_iota(jnp.int32, (1, 1024), 1) % 256 + c * 256
            seen = seen & (key <= here.astype(jnp.float32))
        s = jnp.dot(keys, qbuf[...], preferred_element_type=jnp.float32)
        s = jnp.where(seen, s, -1e30)
        new = jnp.max(s, axis=0, keepdims=True)
        if not first:
            old = m_ref[...]
            new = jnp.maximum(old, new)
        p = jnp.exp((s - new) * scale)
        total = jnp.sum(p, axis=0, keepdims=True)
        part = jnp.dot(vals, p.astype(jnp.bfloat16), preferred_element_type=jnp.float32)
        if first:
            l_ref[...] = total
            o_ref[...] = part
        else:
            alpha = jnp.exp((old - new) * scale)
            l_ref[...] = l_ref[...] * alpha + total
            o_ref[...] = o_ref[...] * alpha + part
        m_ref[...] = new

    def attend(r):
        if r == 0:
            KV.sib_wait(x, 0)
            chunk(x, zlo, True)
            return
        todo = []
        if 1 <= r <= 3:
            b = KV.block(r)
            KV.sib_wait(x, r)
            todo.append((x, b, b < zlo))
        if 1 <= r <= 4:
            KV.sib_wait(xm, r - 1)
            todo.append((x - 1, KV.block(r - 1), x >= 1))
        if 2 <= r <= 5:
            b = KV.block(r - 2)
            KV.sib_wait(xo, r - 2)
            todo.append((x - 2, b, (x >= 2) & (b >= zlo)))

        @pl.loop(0, len(todo))
        def _(i):
            x_, b, cond = todo[-1]
            for j in range(len(todo) - 1):
                x_ = jnp.where(i == j, todo[j][0], x_)
                b = jnp.where(i == j, todo[j][1], b)
                cond = ((i == j) & todo[j][2]) | ((i != j) & cond)

            @pl.when(cond)
            def _():
                chunk(x_, b, False)

    def finish():
        for h in range(4):
            lanes = slice(h * 256, (h + 1) * 256)
            att_out[:, h * 128 : (h + 1) * 128] = jnp.transpose(
                o_ref[:, lanes] / l_ref[0:1, lanes]
            ).astype(jnp.bfloat16)
            lse_out[h : h + 1, :] = m_ref[0:1, lanes] * scale + jnp.log(l_ref[0:1, lanes])

    acc_b[...] = jnp.zeros_like(acc_b)

    A.z_first(1)
    B.x_first(1)
    A.z_first(0)
    B.z_first(1)
    hy_send(1)
    hy_send(0)
    y_fwd(1, zhi, 1)
    small_two()
    A.x_first(0)
    B.x_first(0)
    B.x_fwd(0, 1)
    B.z_first(0)
    A.x_fwd(0, 0)
    hz_send(0)
    hz_send(1)
    A.z_step(1, 1)
    A.x_first(1)
    B.z_step(1, 1)
    A.z_step(1, 0)
    A.z_step(2, 0)
    A.opp_step(0, 0)
    A.x_fwd(2, 0)
    y_fwd(0, zhi, 0)
    B.x_fwd(0, 0)
    B.x_rest(0)
    relay(0)
    B.z_step(1, 0)
    B.x_fwd(1, 1)
    A.x_fwd(1, 0)
    A.x_rest(1)
    A.z_step(2, 1)
    A.x_fwd(1, 1)
    relay(1)
    B.x_fwd(1, 0)
    A.z_step(3, 0)
    y_end(0, zhi, 0)
    A.z_step(3, 1)
    A.opp_step(1, 1)
    A.opp_step(1, 0)
    cross(0)
    A.x_fwd(2, 1)
    small_three()
    A.opp_step(2, 0)
    B.z_step(2, 0)
    A.x_fwd(0, 1)
    cross(1)
    sib_all(A, 1)
    A.x_rest(2)
    A.x_fwd(3, 0)
    y_end(1, zhi, 1)
    B.opp_step(1, 0)
    own_squares()
    A.x_fwd(3, 1)
    B.z_step(2, 1)
    y_fwd(2, 1 - zhi, 0)
    B.z_step(3, 0)
    B.z_step(3, 1)
    B.opp_step(1, 1)
    A.opp_step(0, 1)
    A.x_rest(3)
    A.opp_step(3, 1)
    A.opp_step(2, 1)
    y_fwd(3, 1 - zhi, 1)
    tables()
    sib_all(A, 2)
    B.x_fwd(3, 0)
    A.opp_step(3, 0)
    A.x_rest(0)
    B.x_fwd(2, 1)
    sib_all(A, 0)
    sib_all(A, 3)
    y_end(2, 1 - zhi, 0)
    normalise(0)
    B.opp_step(0, 1)
    y_end(3, 1 - zhi, 1)
    keys_values(0)
    B.opp_step(0, 0)
    KV.z_first(0)
    B.x_fwd(2, 0)
    B.x_fwd(3, 1)
    normalise(1)
    B.x_rest(3)
    keys_values(1)
    B.x_rest(2)
    sib_all(B, 0)
    multiply(B, acc_b, nbuf, 0, 512)
    KV.x_first(0)
    KV.z_first(1)
    B.opp_step(3, 0)
    KV.x_first(1)
    B.opp_step(3, 1)
    B.x_rest(1)
    KV.z_step(2, 1)
    KV.z_step(2, 0)
    KV.z_step(1, 0)
    sib_all(B, 3)
    multiply(B, acc_b, nbuf, 3, 512)
    sib_all(B, 1)
    multiply(B, acc_b, nbuf, 1, 512)
    KV.x_fwd(0, 0)
    B.opp_step(2, 1)
    KV.z_step(1, 1)
    KV.x_fwd(2, 1)
    B.opp_step(2, 0)
    KV.x_fwd(0, 1)
    KV.z_step(3, 0)
    KV.x_fwd(1, 0)
    KV.x_rest(0)
    KV.opp_step(0, 1)
    KV.x_fwd(2, 0)
    KV.opp_step(2, 1)
    KV.x_fwd(1, 1)
    sib_all(B, 2)
    multiply(B, acc_b, nbuf, 2, 512)
    KV.z_step(3, 1)
    KV.opp_step(0, 0)
    queries()
    KV.x_rest(1)
    KV.x_rest(2)
    attend(0)
    KV.opp_step(1, 1)
    attend(2)
    KV.x_fwd(3, 1)
    KV.x_fwd(3, 0)
    KV.opp_step(1, 0)
    attend(1)
    KV.x_rest(3)
    KV.opp_step(2, 0)
    attend(3)
    KV.opp_step(3, 0)
    KV.opp_step(3, 1)
    attend(4)
    attend(5)
    finish()

    for cond, d in sent:
        if cond is None:
            d.wait_send()
        else:
            @pl.when(cond)
            def _(d=d):
                d.wait_send()


def on_device(hidden, gain, w_query, w_key, w_value, doc_ids):
    bf, f32 = jnp.bfloat16, jnp.float32
    hid = hidden.reshape(2, 2, 64, 1024)
    tile = doc_ids.reshape(2, 128)
    gains = gain.reshape(8, 128)
    freq = np.exp(np.arange(64, dtype=np.float32) * np.float32(-2.0 * log_theta / 128))
    freq = jnp.asarray(np.tile(np.concatenate([freq, freq])[None], (8, 1)).astype(np.float32))
    dma = pltpu.SemaphoreType.DMA
    any_, vm = pl.BlockSpec(memory_space=pl.ANY), pl.BlockSpec(memory_space=pltpu.VMEM)
    mixed, cache, sums = pl.pallas_call(
        fused,
        out_shape=(
            jax.ShapeDtypeStruct((256, 512), bf),
            jax.ShapeDtypeStruct((2, 256, 128), bf),
            jax.ShapeDtypeStruct((4, 256), f32),
        ),
        in_specs=[any_] * 6 + [vm],
        out_specs=(vm, vm, vm),
        scratch_shapes=[
            pltpu.VMEM((8, 2, 2, 64, 1024), bf),
            pltpu.VMEM((2, 2, 64, 1024), bf),
            pltpu.VMEM((4, 256, 2048), bf),
            pltpu.VMEM((2, 4, 4, 2, 128, 256), bf),
            pltpu.VMEM((2, 4, 4, 2, 128, 512), bf),
            pltpu.VMEM((2, 4, 4, 2, 2, 128, 128), bf),
            pltpu.VMEM((2, 4, 4, 2, 128), jnp.int32),
            pltpu.VMEM((4, 2, 8, 128), bf),
            pltpu.VMEM((256, 512), f32),
            pltpu.VMEM((128, 1024), bf),
            pltpu.VMEM((256, 128), f32),
            pltpu.VMEM((256, 128), f32),
            pltpu.VMEM((1, 1024), f32),
            pltpu.VMEM((1, 1024), f32),
            pltpu.VMEM((1, 1024), f32),
            pltpu.VMEM((128, 1024), f32),
            dma((6,)), dma((11,)), dma((11,)), dma((2, 2, 2)), dma((2, 2, 2)),
            dma((4, 2, 2)), dma((4, 2, 2)), dma((4, 2)), dma((4, 2)),
        ]
        + [
            dma((2, 4, 2)), dma((4, 2)), dma((2, 4, 2)), dma((2, 4, 2)),
            dma((2, 4)), dma((2, 4)), dma((4, 4, 2)), dma((4, 4, 2)),
        ] * 3,
        compiler_params=pltpu.CompilerParams(
            collective_id=0, has_side_effects=True, vmem_limit_bytes=62 * 1024 * 1024
        ),
        name="fused",
    )(
        hid, gains, w_query.reshape(2, 128, 512), w_key.reshape(2, 128, 128),
        w_value.reshape(2, 128, 128), tile, freq,
    )
    return mixed, cache, sums


def solution(mesh):
    in_specs = (P("seq", "kv"), P("kv"), P("seq", "kv"), P("seq", "kv"), P("seq", "kv"), P("seq"))
    out_specs = (P("seq", "kv"), P(None, "seq", "kv"), P("kv", "seq"))
    return jax.shard_map(
        on_device, mesh=mesh, in_specs=in_specs, out_specs=out_specs, check_vma=False
    )
```

```python
import functools

import jax
import jax.numpy as jnp
import numpy as np
from jax import lax
from jax.experimental import pallas as pl
from jax.experimental.pallas import tpu as pltpu
from jax.sharding import PartitionSpec as P

eps = 1e-05
log_theta = 13.122363377404328
MESH = pl.DeviceIdType.MESH
NX, NZ, NY, NH = 4, 4, 4, 2
DOCS = 17


def fused(
    hid_in, gain_in, wq_in, wk_in, wv_in, ids_in, freq_in,
    att_out, cache_out, lse_out,
    hbuf, rbuf, nbuf, abuf, bbuf, kvbuf, ibuf, gbuf, acc_b, qbuf, cosb, sinb, startr, m_ref, l_ref, o_ref,
    loc_sem, small_s, small_r, hz_s, hz_r, hy_s, hy_r, hf_s, hf_r,
    az_s, az_r, ax_s, ax_r, af_s, af_r, ac_s, ac_r,
    bz_s, bz_r, bx_s, bx_r, bf_s, bf_r, bc_s, bc_r,
    kz_s, kz_r, kx_s, kx_r, kf_s, kf_r, kc_s, kc_r,
):
    kv = lax.axis_index("kv")
    seq = lax.axis_index("seq")
    y, zhi = kv // 2, kv % 2
    c = seq % 2
    zlo = (seq // 2) % 4
    x = seq // 8
    zz = zhi * 4 + zlo

    def at(x_=None, y_=None, zlo_=None, zhi_=None, c_=None):
        x_ = x if x_ is None else x_
        y_ = y if y_ is None else y_
        zlo_ = zlo if zlo_ is None else zlo_
        zhi_ = zhi if zhi_ is None else zhi_
        c_ = c if c_ is None else c_
        return (y_ * 2 + zhi_, (x_ * 4 + zlo_) * 2 + c_)

    def ring_z(step):
        z_ = (zz + 8 + step) % 8
        return z_ % 4, z_ // 4

    xp, xm, xo = (x + 1) % 4, (x + 3) % 4, (x + 2) % 4
    yp, ym, yo = (y + 1) % 4, (y + 3) % 4, (y + 2) % 4
    up_lo, up_hi = ring_z(2)
    dn_lo, dn_hi = ring_z(-2)
    sib = at(c_=1 - c)
    dev_xp, dev_xm = at(x_=xp), at(x_=xm)
    dev_yp, dev_ym = at(y_=yp), at(y_=ym)
    dev_up2, dev_dn2 = at(zlo_=up_lo, zhi_=up_hi), at(zlo_=dn_lo, zhi_=dn_hi)
    dev_zu, dev_zd = at(zlo_=(zlo + 1) % 4), at(zlo_=(zlo + 3) % 4)
    dev_pair = at(zhi_=1 - zhi)

    def rc(src, dst, ss, rs, dev):
        return pltpu.make_async_remote_copy(
            src_ref=src, dst_ref=dst, send_sem=ss, recv_sem=rs, device_id=dev, device_id_type=MESH
        )

    sent = []

    def send(src, dst, ss, rs, dev):
        d = rc(src, dst, ss, rs, dev)
        d.start()
        sent.append((None, d))

    def send_if(cond, src, dst, ss, rs, dev):
        d = rc(src, dst, ss, rs, dev)

        @pl.when(cond)
        def _():
            d.start()

        sent.append((cond, d))

    def got(ref, ss, rs):
        rc(ref, ref, ss, rs, sib).wait_recv()

    amine = abuf.at[c, x, zlo]
    hmine = hbuf.at[kv]
    locals_ = [
        pltpu.make_async_copy(wq_in, bbuf.at[c, x, zlo], loc_sem.at[0]),
        pltpu.make_async_copy(wk_in, amine.at[:, :, pl.ds(0, 128)], loc_sem.at[1]),
        pltpu.make_async_copy(wv_in, amine.at[:, :, pl.ds(128, 128)], loc_sem.at[2]),
        pltpu.make_async_copy(hid_in, hmine, loc_sem.at[3]),
        pltpu.make_async_copy(ids_in, ibuf.at[c, x, zlo], loc_sem.at[4]),
        pltpu.make_async_copy(gain_in, gbuf.at[y, zhi], loc_sem.at[5]),
    ]
    for d in locals_:
        d.start()

    barrier = pltpu.get_barrier_semaphore()
    peers = [sib, dev_pair, dev_up2, dev_dn2]
    for d in (1, 2, 3):
        peers += [at(x_=(x + d) % 4), at(y_=(y + d) % 4), at(zlo_=(zlo + d) % 4)]
    for dev in peers:
        pl.semaphore_signal(barrier, inc=1, device_id=dev, device_id_type=MESH)
    for d in locals_:
        d.wait()
    pl.semaphore_wait(barrier, len(peers))

    for d in (1, 2, 3):
        t = ibuf.at[c, x, zlo]
        send(t, t, small_s.at[d - 1], small_r.at[d - 1], at(zlo_=(zlo + d) % 4))
    t = gbuf.at[y, zhi]
    send(t, t, small_s.at[3], small_r.at[3], dev_pair)

    class Gather:
        def __init__(self, buf, zs, zr, xs, xr, fs, fr, cs, cr, back_only=False):
            self.back_only = back_only
            self.buf, self.zs, self.zr, self.xs, self.xr = buf, zs, zr, xs, xr
            self.fs, self.fr, self.cs, self.cr = fs, fr, cs, cr

        def block(self, r):
            if r == 0:
                return zlo
            mid = {1: (0, 3), 2: (2, 1), 3: (3, 0)}[r]
            return jnp.where(
                zlo == 0, r, jnp.where(zlo == 3, 3 - r, jnp.where(zlo == 1, mid[0], mid[1]))
            )

        def to_sib(self, x_, b, h):
            s = self.buf.at[c, x_, b, h]
            send(s, s, self.cs.at[x_, b, h], self.cr.at[x_, b, h], sib)

        def z_part(self, b, h):
            s = self.buf.at[c, x, b, h]
            send_if((zlo < 3) & (b <= zlo), s, s, self.zs.at[0, b, h], self.zr.at[b, h], dev_zu)
            send_if((zlo > 0) & (b >= zlo), s, s, self.zs.at[1, b, h], self.zr.at[b, h], dev_zd)

        def x_part(self, b, h):
            s = self.buf.at[c, x, b, h]
            send(s, s, self.xs.at[0, b, h], self.xr.at[0, b, h], dev_xp)
            if h == 1 or not self.back_only:
                send(s, s, self.xs.at[1, b, h], self.xr.at[1, b, h], dev_xm)
            self.to_sib(x, b, h)

        def z_first(self, h):
            self.z_part(zlo, h)

        def x_first(self, h):
            self.x_part(zlo, h)

        def z_step(self, r, h):
            b = self.block(r)
            got(self.buf.at[c, x, b, h], self.zs.at[0, b, h], self.zr.at[b, h])
            self.z_part(b, h)
            self.x_part(b, h)

        def x_fwd(self, r, h):
            b = self.block(r)
            x_, dev = ((xm, dev_xp), (xp, dev_xm))[h]
            t = self.buf.at[c, x_, b, h]
            got(t, self.xs.at[h, b, h], self.xr.at[h, b, h])
            send(t, t, self.fs.at[h, b], self.fr.at[h, b], dev)
            if h == 0 or not self.back_only:
                self.to_sib(x_, b, h)

        def x_rest(self, r):
            b = self.block(r)
            got(self.buf.at[c, xm, b, 1], self.xs.at[0, b, 1], self.xr.at[0, b, 1])
            self.to_sib(xm, b, 1)
            if not self.back_only:
                got(self.buf.at[c, xp, b, 0], self.xs.at[1, b, 0], self.xr.at[1, b, 0])
                self.to_sib(xp, b, 0)

        def opp_step(self, r, h):
            b = self.block(r)
            t = self.buf.at[c, xo, b, h]
            got(t, self.fs.at[h, b], self.fr.at[h, b])
            self.to_sib(xo, b, h)

        def sib_wait(self, x_, r):
            b = self.block(r)
            for h in (0, 1):
                got(self.buf.at[1 - c, x_, b, h], self.cs.at[x_, b, h], self.cr.at[x_, b, h])

    A = Gather(abuf, az_s, az_r, ax_s, ax_r, af_s, af_r, ac_s, ac_r)
    B = Gather(bbuf, bz_s, bz_r, bx_s, bx_r, bf_s, bf_r, bc_s, bc_r)
    KV = Gather(kvbuf, kz_s, kz_r, kx_s, kx_r, kf_s, kf_r, kc_s, kc_r, True)

    def y_part(g, zh, h, way, p):
        t = hbuf.at[y * 2 + zh, p, h]
        send(t, t, hy_s.at[g, way, h], hy_r.at[g, way, h], (dev_yp, dev_ym)[way])

    def y_fwd(g, zh, p):
        t = hbuf.at[ym * 2 + zh, p, 0]
        got(t, hy_s.at[g, 0, 0], hy_r.at[g, 0, 0])
        send(t, t, hf_s.at[g, 0], hf_r.at[g, 0], dev_yp)
        t = hbuf.at[yp * 2 + zh, p, 1]
        got(t, hy_s.at[g, 1, 1], hy_r.at[g, 1, 1])
        send(t, t, hf_s.at[g, 1], hf_r.at[g, 1], dev_ym)

    def y_end(g, zh, p):
        got(hbuf.at[ym * 2 + zh, p, 1], hy_s.at[g, 0, 1], hy_r.at[g, 0, 1])
        got(hbuf.at[yp * 2 + zh, p, 0], hy_s.at[g, 1, 0], hy_r.at[g, 1, 0])
        for h in (0, 1):
            got(hbuf.at[yo * 2 + zh, p, h], hf_s.at[g, h], hf_r.at[g, h])

    def hz_send(p):
        for way, dev in ((0, dev_up2), (1, dev_dn2)):
            send(
                hmine.at[p, way], rbuf.at[p, way],
                hz_s.at[0, way, p], hz_r.at[0, way, p], dev,
            )

    def relay(p):
        for way, hi, dev in ((0, dn_hi, dev_up2), (1, up_hi, dev_dn2)):
            t = rbuf.at[p, way]
            got(t, hz_s.at[0, way, p], hz_r.at[0, way, p])
            send(
                t, hbuf.at[y * 2 + hi, p, way],
                hz_s.at[1, way, p], hz_r.at[1, way, p], dev,
            )

    def cross(p):
        for h in (0, 1):
            t = hbuf.at[y * 2 + 1 - zhi, p, h]
            got(t, hz_s.at[1, h, p], hz_r.at[1, h, p])
            y_part(2 + p, 1 - zhi, h, 0, p)
            y_part(2 + p, 1 - zhi, h, 1, p)

    def hy_send(p):
        for h in (0, 1):
            y_part(p, zhi, h, 0, p)
            y_part(p, zhi, 1 - h, 1, p)

    def small_two():
        for d in (1, 2, 3):
            got(ibuf.at[c, x, (zlo + 4 - d) % 4], small_s.at[d - 1], small_r.at[d - 1])
        got(gbuf.at[y, 1 - zhi], small_s.at[3], small_r.at[3])
        for d in (1, 2, 3):
            t = ibuf.at[c, x]
            send(t, t, small_s.at[3 + d], small_r.at[3 + d], at(x_=(x + d) % 4))
            t = gbuf.at[y]
            send(t, t, small_s.at[6 + d], small_r.at[6 + d], at(y_=(y + d) % 4))

    def small_three():
        for d in (1, 2, 3):
            got(ibuf.at[c, (x + 4 - d) % 4], small_s.at[3 + d], small_r.at[3 + d])
            got(gbuf.at[(y + 4 - d) % 4], small_s.at[6 + d], small_r.at[6 + d])
        t = ibuf.at[c]
        send(t, t, small_s.at[10], small_r.at[10], sib)

    def squares(p, zh, total):
        def one(i, total):
            for j in range(8):
                h = hbuf[i * 2 + zh, p, :, :, j * 128 : (j + 1) * 128].reshape(128, 128)
                h = h.astype(jnp.float32)
                total = total + h * h
            return total

        return lax.fori_loop(0, 4, one, total)

    totals = [None, None]

    def own_squares():
        for p in (0, 1):
            totals[p] = squares(p, zhi, jnp.zeros((128, 128), jnp.float32))

    def multiply(G, acc, nbuf_, r, width):
        b = G.block(r)
        w = G.buf[:, :, b].reshape(2048, width)
        acc[...] += jnp.dot(nbuf_[b], w, preferred_element_type=jnp.float32)

    def sib_all(G, r):
        for x_ in (x, xm, xp, xo):
            G.sib_wait(x_, r)

    def turn(u, rows=slice(0, 256)):
        return u * cosb[rows, :] + pltpu.roll(u, 64, 1) * sinb[rows, :]

    def tables():
        got(ibuf.at[1 - c], small_s.at[10], small_r.at[10])
        every = ibuf[...].reshape(32, 2, 128)
        mine = ibuf[c, x, zlo].astype(jnp.float32)
        idc = jnp.concatenate(
            [jnp.transpose(jnp.broadcast_to(mine[i : i + 1, :], (128, 128))) for i in (0, 1)], axis=0
        )
        start = jnp.zeros((256, 128), jnp.float32)
        start_row = jnp.zeros((2, 128), jnp.float32)
        for d in range(DOCS - 1):
            hits = jnp.sum(jnp.where(every == d, 1.0, 0.0), axis=0)
            held = jnp.sum(jnp.sum(hits, axis=0, keepdims=True), axis=1, keepdims=True)
            start = start + jnp.where(idc > d, held, 0.0)
            start_row = start_row + jnp.where(mine > d, held, 0.0)
        for i in (0, 1):
            for h in range(4):
                startr[0:1, h * 256 + i * 128 : h * 256 + (i + 1) * 128] = start_row[i : i + 1, :]
        row = lax.broadcasted_iota(jnp.int32, (256, 128), 0).astype(jnp.float32)
        tok = row + (seq * 256).astype(jnp.float32)
        angle = (tok - start) * freq_in[0:1, :]
        lane = lax.broadcasted_iota(jnp.int32, (256, 128), 1)
        cosb[...] = jnp.cos(angle)
        sinb[...] = jnp.where(lane < 64, -1.0, 1.0) * jnp.sin(angle)

    def normalise(p):
        total = squares(p, 1 - zhi, totals[p])
        factor = lax.rsqrt(jnp.sum(total, axis=1, keepdims=True) * (1.0 / 8192.0) + eps)
        factor = jnp.broadcast_to(factor, (128, 128))

        @pl.loop(0, 8)
        def _(k):
            g = gbuf[k // 2, k % 2].astype(jnp.float32)
            for i in range(8):
                h = hbuf[k, p, :, :, i * 128 : (i + 1) * 128].reshape(128, 128)
                lane = pl.multiple_of(((i // 2) % 2 * 4 + k // 2) * 256 + (i % 2) * 128, 128)
                nbuf[(k % 2) * 2 + i // 4, p * 128 : (p + 1) * 128, pl.ds(lane, 128)] = (
                    h.astype(jnp.float32) * factor * g[i : i + 1, :]
                ).astype(jnp.bfloat16)

    def keys_values(p):
        rows = slice(p * 128, (p + 1) * 128)

        sums = jnp.zeros((128, 256), jnp.float32)
        for b in range(4):
            w = abuf[:, :, b].reshape(2048, 256)
            sums = sums + jnp.dot(nbuf[b, rows, :], w, preferred_element_type=jnp.float32)
        kmine = turn(sums[:, 0:128], rows).astype(jnp.bfloat16)
        vmine = sums[:, 128:256].astype(jnp.bfloat16)
        kvbuf[c, x, zlo, p, 0] = kmine
        kvbuf[c, x, zlo, p, 1] = vmine
        cache_out[0, rows, :] = kmine
        cache_out[1, rows, :] = vmine

    def queries():
        for h in range(4):
            q = turn(acc_b[:, h * 128 : (h + 1) * 128])
            qbuf[:, h * 256 : (h + 1) * 256] = jnp.transpose(q).astype(jnp.bfloat16)

    scale = 128 ** (-0.5)

    def chunk(x_, b, first):
        base = ((x_ * 4 + b) * 512).astype(jnp.float32)
        keys = kvbuf[:, x_, b, :, 0].reshape(512, 128)
        vals = jnp.transpose(kvbuf[:, x_, b, :, 1].reshape(512, 128))
        key = lax.broadcasted_iota(jnp.int32, (512, 1024), 0).astype(jnp.float32)
        seen = key >= startr[...] - base
        if first:
            here = lax.broadcasted_iota(jnp.int32, (1, 1024), 1) % 256 + c * 256
            seen = seen & (key <= here.astype(jnp.float32))
        s = jnp.dot(keys, qbuf[...], preferred_element_type=jnp.float32)
        s = jnp.where(seen, s, -1e30)
        new = jnp.max(s, axis=0, keepdims=True)
        if not first:
            old = m_ref[...]
            new = jnp.maximum(old, new)
        p = jnp.exp((s - new) * scale)
        total = jnp.sum(p, axis=0, keepdims=True)
        part = jnp.dot(vals, p.astype(jnp.bfloat16), preferred_element_type=jnp.float32)
        if first:
            l_ref[...] = total
            o_ref[...] = part
        else:
            alpha = jnp.exp((old - new) * scale)
            l_ref[...] = l_ref[...] * alpha + total
            o_ref[...] = o_ref[...] * alpha + part
        m_ref[...] = new

    def attend(r):
        if r == 0:
            KV.sib_wait(x, 0)
            chunk(x, zlo, True)
            return
        todo = []
        if 1 <= r <= 3:
            b = KV.block(r)
            KV.sib_wait(x, r)
            todo.append((x, b, b < zlo))
        if 1 <= r <= 4:
            KV.sib_wait(xm, r - 1)
            todo.append((x - 1, KV.block(r - 1), x >= 1))
        if 2 <= r <= 5:
            b = KV.block(r - 2)
            KV.sib_wait(xo, r - 2)
            todo.append((x - 2, b, (x >= 2) & (b >= zlo)))

        @pl.loop(0, len(todo))
        def _(i):
            x_, b, cond = todo[-1]
            for j in range(len(todo) - 1):
                x_ = jnp.where(i == j, todo[j][0], x_)
                b = jnp.where(i == j, todo[j][1], b)
                cond = ((i == j) & todo[j][2]) | ((i != j) & cond)

            @pl.when(cond)
            def _():
                chunk(x_, b, False)

    def finish():
        for h in range(4):
            lanes = slice(h * 256, (h + 1) * 256)
            att_out[:, h * 128 : (h + 1) * 128] = jnp.transpose(
                o_ref[:, lanes] / l_ref[0:1, lanes]
            ).astype(jnp.bfloat16)
            lse_out[h : h + 1, :] = m_ref[0:1, lanes] * scale + jnp.log(l_ref[0:1, lanes])

    acc_b[...] = jnp.zeros_like(acc_b)

    A.z_first(1)
    B.x_first(1)
    A.z_first(0)
    B.z_first(1)
    hy_send(1)
    hy_send(0)
    y_fwd(1, zhi, 1)
    small_two()
    A.x_first(0)
    B.x_first(0)
    B.x_fwd(0, 1)
    B.z_first(0)
    A.x_fwd(0, 0)
    hz_send(0)
    hz_send(1)
    A.z_step(1, 1)
    A.x_first(1)
    B.z_step(1, 1)
    A.z_step(1, 0)
    A.z_step(2, 0)
    A.opp_step(0, 0)
    A.x_fwd(2, 0)
    y_fwd(0, zhi, 0)
    B.x_fwd(0, 0)
    B.x_rest(0)
    relay(0)
    B.z_step(1, 0)
    B.x_fwd(1, 1)
    A.x_fwd(1, 0)
    A.x_rest(1)
    A.z_step(2, 1)
    A.x_fwd(1, 1)
    relay(1)
    B.x_fwd(1, 0)
    A.z_step(3, 0)
    y_end(0, zhi, 0)
    A.z_step(3, 1)
    A.opp_step(1, 1)
    A.opp_step(1, 0)
    cross(0)
    A.x_fwd(2, 1)
    small_three()
    A.opp_step(2, 0)
    B.z_step(2, 0)
    A.x_fwd(0, 1)
    cross(1)
    sib_all(A, 1)
    A.x_rest(2)
    A.x_fwd(3, 0)
    y_end(1, zhi, 1)
    B.opp_step(1, 0)
    own_squares()
    A.x_fwd(3, 1)
    B.z_step(2, 1)
    y_fwd(2, 1 - zhi, 0)
    B.z_step(3, 0)
    B.z_step(3, 1)
    B.opp_step(1, 1)
    A.opp_step(0, 1)
    A.x_rest(3)
    A.opp_step(3, 1)
    A.opp_step(2, 1)
    y_fwd(3, 1 - zhi, 1)
    tables()
    sib_all(A, 2)
    B.x_fwd(3, 0)
    A.opp_step(3, 0)
    A.x_rest(0)
    B.x_fwd(2, 1)
    sib_all(A, 0)
    sib_all(A, 3)
    y_end(2, 1 - zhi, 0)
    normalise(0)
    B.opp_step(0, 1)
    y_end(3, 1 - zhi, 1)
    keys_values(0)
    B.opp_step(0, 0)
    KV.z_first(0)
    B.x_fwd(2, 0)
    B.x_fwd(3, 1)
    normalise(1)
    B.x_rest(3)
    keys_values(1)
    B.x_rest(2)
    sib_all(B, 0)
    multiply(B, acc_b, nbuf, 0, 512)
    KV.x_first(0)
    KV.z_first(1)
    B.opp_step(3, 0)
    KV.x_first(1)
    B.opp_step(3, 1)
    B.x_rest(1)
    KV.z_step(2, 1)
    KV.z_step(2, 0)
    KV.z_step(1, 0)
    sib_all(B, 3)
    multiply(B, acc_b, nbuf, 3, 512)
    sib_all(B, 1)
    multiply(B, acc_b, nbuf, 1, 512)
    KV.x_fwd(0, 0)
    B.opp_step(2, 1)
    KV.z_step(1, 1)
    KV.x_fwd(2, 1)
    B.opp_step(2, 0)
    KV.x_fwd(0, 1)
    KV.z_step(3, 0)
    KV.x_fwd(1, 0)
    KV.x_rest(0)
    KV.opp_step(0, 1)
    KV.x_fwd(2, 0)
    KV.opp_step(2, 1)
    KV.x_fwd(1, 1)
    sib_all(B, 2)
    multiply(B, acc_b, nbuf, 2, 512)
    KV.z_step(3, 1)
    KV.opp_step(0, 0)
    queries()
    KV.x_rest(1)
    KV.x_rest(2)
    attend(0)
    KV.opp_step(1, 1)
    attend(2)
    KV.x_fwd(3, 1)
    KV.x_fwd(3, 0)
    KV.opp_step(1, 0)
    attend(1)
    KV.x_rest(3)
    KV.opp_step(2, 0)
    attend(3)
    KV.opp_step(3, 0)
    KV.opp_step(3, 1)
    attend(4)
    attend(5)
    finish()

    for cond, d in sent:
        if cond is None:
            d.wait_send()
        else:
            @pl.when(cond)
            def _(d=d):
                d.wait_send()


def put(*refs):
    for source, target in zip(refs[:3], refs[3:]):
        target[...] = source[...]


def on_device(hidden, gain, w_query, w_key, w_value, doc_ids):
    bf, f32 = jnp.bfloat16, jnp.float32
    hid = hidden.reshape(2, 2, 64, 1024)
    tile = doc_ids.reshape(2, 128)
    gains = gain.reshape(8, 128)
    freq = np.exp(np.arange(64, dtype=np.float32) * np.float32(-2.0 * log_theta / 128))
    freq = jnp.asarray(np.tile(np.concatenate([freq, freq])[None], (8, 1)).astype(np.float32))
    dma = pltpu.SemaphoreType.DMA
    any_, vm = pl.BlockSpec(memory_space=pl.ANY), pl.BlockSpec(memory_space=pltpu.VMEM)
    mixed, cache, sums = pl.pallas_call(
        fused,
        out_shape=(
            jax.ShapeDtypeStruct((256, 512), bf),
            jax.ShapeDtypeStruct((2, 256, 128), bf),
            jax.ShapeDtypeStruct((4, 256), f32),
        ),
        in_specs=[any_] * 6 + [vm],
        out_specs=(vm, vm, vm),
        scratch_shapes=[
            pltpu.VMEM((8, 2, 2, 64, 1024), bf),
            pltpu.VMEM((2, 2, 64, 1024), bf),
            pltpu.VMEM((4, 256, 2048), bf),
            pltpu.VMEM((2, 4, 4, 2, 128, 256), bf),
            pltpu.VMEM((2, 4, 4, 2, 128, 512), bf),
            pltpu.VMEM((2, 4, 4, 2, 2, 128, 128), bf),
            pltpu.VMEM((2, 4, 4, 2, 128), jnp.int32),
            pltpu.VMEM((4, 2, 8, 128), bf),
            pltpu.VMEM((256, 512), f32),
            pltpu.VMEM((128, 1024), bf),
            pltpu.VMEM((256, 128), f32),
            pltpu.VMEM((256, 128), f32),
            pltpu.VMEM((1, 1024), f32),
            pltpu.VMEM((1, 1024), f32),
            pltpu.VMEM((1, 1024), f32),
            pltpu.VMEM((128, 1024), f32),
            dma((6,)), dma((11,)), dma((11,)), dma((2, 2, 2)), dma((2, 2, 2)),
            dma((4, 2, 2)), dma((4, 2, 2)), dma((4, 2)), dma((4, 2)),
        ]
        + [
            dma((2, 4, 2)), dma((4, 2)), dma((2, 4, 2)), dma((2, 4, 2)),
            dma((2, 4)), dma((2, 4)), dma((4, 4, 2)), dma((4, 4, 2)),
        ] * 3,
        compiler_params=pltpu.CompilerParams(
            collective_id=0, has_side_effects=True, vmem_limit_bytes=62 * 1024 * 1024
        ),
        name="fused",
    )(
        hid, gains, w_query.reshape(2, 128, 512), w_key.reshape(2, 128, 128),
        w_value.reshape(2, 128, 128), tile, freq,
    )
    return pl.pallas_call(
        put,
        out_shape=tuple(jax.ShapeDtypeStruct(t.shape, t.dtype) for t in (mixed, cache, sums)),
        in_specs=[vm] * 3,
        out_specs=(vm,) * 3,
        name="put",
    )(mixed, cache, sums)


def solution(mesh):
    in_specs = (P("seq", "kv"), P("kv"), P("seq", "kv"), P("seq", "kv"), P("seq", "kv"), P("seq"))
    out_specs = (P("seq", "kv"), P(None, "seq", "kv"), P("kv", "seq"))
    return jax.shard_map(
        on_device, mesh=mesh, in_specs=in_specs, out_specs=out_specs, check_vma=False
    )
```

```python
import functools

import jax
import jax.numpy as jnp
import numpy as np
from jax import lax
from jax.experimental import pallas as pl
from jax.experimental.pallas import tpu as pltpu
from jax.sharding import PartitionSpec as P

eps = 1e-05
log_theta = 13.122363377404328
log2_e = 1.4426950408889634
MESH = pl.DeviceIdType.MESH
NX, NZ, NY, NH = 4, 4, 4, 2
DOCS = 17


def fused(
    hid_in, gain_in, wq_in, wk_in, wv_in, ids_in, freq_in,
    att_out, cache_out, lse_out,
    hbuf, rbuf, nbuf, abuf, bbuf, kvbuf, ibuf, gbuf, acc_b, qbuf, cosb, sinb, startr, m_ref, l_ref, o_ref,
    loc_sem, small_s, small_r, hz_s, hz_r, hy_s, hy_r, hf_s, hf_r,
    az_s, az_r, ax_s, ax_r, af_s, af_r, ac_s, ac_r,
    bz_s, bz_r, bx_s, bx_r, bf_s, bf_r, bc_s, bc_r,
    kz_s, kz_r, kx_s, kx_r, kf_s, kf_r, kc_s, kc_r,
):
    kv = lax.axis_index("kv")
    seq = lax.axis_index("seq")
    y, zhi = kv // 2, kv % 2
    c = seq % 2
    zlo = (seq // 2) % 4
    x = seq // 8
    zz = zhi * 4 + zlo

    def at(x_=None, y_=None, zlo_=None, zhi_=None, c_=None):
        x_ = x if x_ is None else x_
        y_ = y if y_ is None else y_
        zlo_ = zlo if zlo_ is None else zlo_
        zhi_ = zhi if zhi_ is None else zhi_
        c_ = c if c_ is None else c_
        return (y_ * 2 + zhi_, (x_ * 4 + zlo_) * 2 + c_)

    def ring_z(step):
        z_ = (zz + 8 + step) % 8
        return z_ % 4, z_ // 4

    xp, xm, xo = (x + 1) % 4, (x + 3) % 4, (x + 2) % 4
    yp, ym, yo = (y + 1) % 4, (y + 3) % 4, (y + 2) % 4
    up_lo, up_hi = ring_z(2)
    dn_lo, dn_hi = ring_z(-2)
    sib = at(c_=1 - c)
    dev_xp, dev_xm = at(x_=xp), at(x_=xm)
    dev_yp, dev_ym = at(y_=yp), at(y_=ym)
    dev_up2, dev_dn2 = at(zlo_=up_lo, zhi_=up_hi), at(zlo_=dn_lo, zhi_=dn_hi)
    dev_zu, dev_zd = at(zlo_=(zlo + 1) % 4), at(zlo_=(zlo + 3) % 4)
    dev_pair = at(zhi_=1 - zhi)

    def rc(src, dst, ss, rs, dev):
        return pltpu.make_async_remote_copy(
            src_ref=src, dst_ref=dst, send_sem=ss, recv_sem=rs, device_id=dev, device_id_type=MESH
        )

    sent = []

    def send(src, dst, ss, rs, dev):
        d = rc(src, dst, ss, rs, dev)
        d.start()
        sent.append((None, d))

    def send_if(cond, src, dst, ss, rs, dev):
        d = rc(src, dst, ss, rs, dev)

        @pl.when(cond)
        def _():
            d.start()

        sent.append((cond, d))

    def got(ref, ss, rs):
        rc(ref, ref, ss, rs, sib).wait_recv()

    amine = abuf.at[c, x, zlo]
    hmine = hbuf.at[kv]
    locals_ = [
        pltpu.make_async_copy(wq_in, bbuf.at[c, x, zlo], loc_sem.at[0]),
        pltpu.make_async_copy(wk_in, amine.at[:, :, pl.ds(0, 128)], loc_sem.at[1]),
        pltpu.make_async_copy(wv_in, amine.at[:, :, pl.ds(128, 128)], loc_sem.at[2]),
        pltpu.make_async_copy(hid_in, hmine, loc_sem.at[3]),
        pltpu.make_async_copy(ids_in, ibuf.at[c, x, zlo], loc_sem.at[4]),
        pltpu.make_async_copy(gain_in, gbuf.at[y, zhi], loc_sem.at[5]),
    ]
    for d in locals_:
        d.start()

    barrier = pltpu.get_barrier_semaphore()
    peers = [sib, dev_pair, dev_up2, dev_dn2]
    for d in (1, 2, 3):
        peers += [at(x_=(x + d) % 4), at(y_=(y + d) % 4), at(zlo_=(zlo + d) % 4)]
    for dev in peers:
        pl.semaphore_signal(barrier, inc=1, device_id=dev, device_id_type=MESH)
    for d in locals_:
        d.wait()
    pl.semaphore_wait(barrier, len(peers))

    for d in (1, 2, 3):
        t = ibuf.at[c, x, zlo]
        send(t, t, small_s.at[d - 1], small_r.at[d - 1], at(zlo_=(zlo + d) % 4))
    t = gbuf.at[y, zhi]
    send(t, t, small_s.at[3], small_r.at[3], dev_pair)

    class Gather:
        def __init__(self, buf, zs, zr, xs, xr, fs, fr, cs, cr, back_only=False):
            self.back_only = back_only
            self.buf, self.zs, self.zr, self.xs, self.xr = buf, zs, zr, xs, xr
            self.fs, self.fr, self.cs, self.cr = fs, fr, cs, cr

        def block(self, r):
            if r == 0:
                return zlo
            mid = {1: (0, 3), 2: (2, 1), 3: (3, 0)}[r]
            return jnp.where(
                zlo == 0, r, jnp.where(zlo == 3, 3 - r, jnp.where(zlo == 1, mid[0], mid[1]))
            )

        def to_sib(self, x_, b, h):
            s = self.buf.at[c, x_, b, h]
            send(s, s, self.cs.at[x_, b, h], self.cr.at[x_, b, h], sib)

        def z_part(self, b, h):
            s = self.buf.at[c, x, b, h]
            send_if((zlo < 3) & (b <= zlo), s, s, self.zs.at[0, b, h], self.zr.at[b, h], dev_zu)
            send_if((zlo > 0) & (b >= zlo), s, s, self.zs.at[1, b, h], self.zr.at[b, h], dev_zd)

        def x_part(self, b, h):
            s = self.buf.at[c, x, b, h]
            send(s, s, self.xs.at[0, b, h], self.xr.at[0, b, h], dev_xp)
            if h == 1 or not self.back_only:
                send(s, s, self.xs.at[1, b, h], self.xr.at[1, b, h], dev_xm)
            self.to_sib(x, b, h)

        def z_first(self, h):
            self.z_part(zlo, h)

        def x_first(self, h):
            self.x_part(zlo, h)

        def z_step(self, r, h):
            b = self.block(r)
            got(self.buf.at[c, x, b, h], self.zs.at[0, b, h], self.zr.at[b, h])
            self.z_part(b, h)
            self.x_part(b, h)

        def x_fwd(self, r, h):
            b = self.block(r)
            x_, dev = ((xm, dev_xp), (xp, dev_xm))[h]
            t = self.buf.at[c, x_, b, h]
            got(t, self.xs.at[h, b, h], self.xr.at[h, b, h])
            send(t, t, self.fs.at[h, b], self.fr.at[h, b], dev)
            if h == 0 or not self.back_only:
                self.to_sib(x_, b, h)

        def x_rest(self, r):
            b = self.block(r)
            got(self.buf.at[c, xm, b, 1], self.xs.at[0, b, 1], self.xr.at[0, b, 1])
            self.to_sib(xm, b, 1)
            if not self.back_only:
                got(self.buf.at[c, xp, b, 0], self.xs.at[1, b, 0], self.xr.at[1, b, 0])
                self.to_sib(xp, b, 0)

        def opp_step(self, r, h):
            b = self.block(r)
            t = self.buf.at[c, xo, b, h]
            got(t, self.fs.at[h, b], self.fr.at[h, b])
            self.to_sib(xo, b, h)

        def sib_wait(self, x_, r):
            b = self.block(r)
            for h in (0, 1):
                got(self.buf.at[1 - c, x_, b, h], self.cs.at[x_, b, h], self.cr.at[x_, b, h])

    A = Gather(abuf, az_s, az_r, ax_s, ax_r, af_s, af_r, ac_s, ac_r)
    B = Gather(bbuf, bz_s, bz_r, bx_s, bx_r, bf_s, bf_r, bc_s, bc_r)
    KV = Gather(kvbuf, kz_s, kz_r, kx_s, kx_r, kf_s, kf_r, kc_s, kc_r, True)

    def y_part(g, zh, h, way, p):
        t = hbuf.at[y * 2 + zh, p, h]
        send(t, t, hy_s.at[g, way, h], hy_r.at[g, way, h], (dev_yp, dev_ym)[way])

    def y_fwd(g, zh, p):
        t = hbuf.at[ym * 2 + zh, p, 0]
        got(t, hy_s.at[g, 0, 0], hy_r.at[g, 0, 0])
        send(t, t, hf_s.at[g, 0], hf_r.at[g, 0], dev_yp)
        t = hbuf.at[yp * 2 + zh, p, 1]
        got(t, hy_s.at[g, 1, 1], hy_r.at[g, 1, 1])
        send(t, t, hf_s.at[g, 1], hf_r.at[g, 1], dev_ym)

    def y_end(g, zh, p):
        got(hbuf.at[ym * 2 + zh, p, 1], hy_s.at[g, 0, 1], hy_r.at[g, 0, 1])
        got(hbuf.at[yp * 2 + zh, p, 0], hy_s.at[g, 1, 0], hy_r.at[g, 1, 0])
        for h in (0, 1):
            got(hbuf.at[yo * 2 + zh, p, h], hf_s.at[g, h], hf_r.at[g, h])

    def hz_send(p):
        for way, dev in ((0, dev_up2), (1, dev_dn2)):
            send(
                hmine.at[p, way], rbuf.at[p, way],
                hz_s.at[0, way, p], hz_r.at[0, way, p], dev,
            )

    def relay(p):
        for way, hi, dev in ((0, dn_hi, dev_up2), (1, up_hi, dev_dn2)):
            t = rbuf.at[p, way]
            got(t, hz_s.at[0, way, p], hz_r.at[0, way, p])
            send(
                t, hbuf.at[y * 2 + hi, p, way],
                hz_s.at[1, way, p], hz_r.at[1, way, p], dev,
            )

    def cross(p):
        for h in (0, 1):
            t = hbuf.at[y * 2 + 1 - zhi, p, h]
            got(t, hz_s.at[1, h, p], hz_r.at[1, h, p])
            y_part(2 + p, 1 - zhi, h, 0, p)
            y_part(2 + p, 1 - zhi, h, 1, p)

    def hy_send(p):
        for h in (0, 1):
            y_part(p, zhi, h, 0, p)
            y_part(p, zhi, 1 - h, 1, p)

    def small_two():
        for d in (1, 2, 3):
            got(ibuf.at[c, x, (zlo + 4 - d) % 4], small_s.at[d - 1], small_r.at[d - 1])
        got(gbuf.at[y, 1 - zhi], small_s.at[3], small_r.at[3])
        for d in (1, 2, 3):
            t = ibuf.at[c, x]
            send(t, t, small_s.at[3 + d], small_r.at[3 + d], at(x_=(x + d) % 4))
            t = gbuf.at[y]
            send(t, t, small_s.at[6 + d], small_r.at[6 + d], at(y_=(y + d) % 4))

    def small_three():
        for d in (1, 2, 3):
            got(ibuf.at[c, (x + 4 - d) % 4], small_s.at[3 + d], small_r.at[3 + d])
            got(gbuf.at[(y + 4 - d) % 4], small_s.at[6 + d], small_r.at[6 + d])
        t = ibuf.at[c]
        send(t, t, small_s.at[10], small_r.at[10], sib)

    def squares(p, zh, total):
        def one(i, total):
            for j in range(8):
                h = hbuf[i * 2 + zh, p, :, :, j * 128 : (j + 1) * 128].reshape(128, 128)
                h = h.astype(jnp.float32)
                total = total + h * h
            return total

        return lax.fori_loop(0, 4, one, total)

    totals = [None, None]

    def own_squares():
        for p in (0, 1):
            totals[p] = squares(p, zhi, jnp.zeros((128, 128), jnp.float32))

    def multiply(G, acc, nbuf_, r, width):
        b = G.block(r)
        w = G.buf[:, :, b].reshape(2048, width)
        acc[...] += jnp.dot(nbuf_[b], w, preferred_element_type=jnp.float32)

    def sib_all(G, r):
        for x_ in (x, xm, xp, xo):
            G.sib_wait(x_, r)

    def turn(u, rows=slice(0, 256)):
        return u * cosb[rows, :] + pltpu.roll(u, 64, 1) * sinb[rows, :]

    def tables():
        got(ibuf.at[1 - c], small_s.at[10], small_r.at[10])
        every = ibuf[...].reshape(32, 2, 128)
        mine = ibuf[c, x, zlo].astype(jnp.float32)
        idc = jnp.concatenate(
            [jnp.transpose(jnp.broadcast_to(mine[i : i + 1, :], (128, 128))) for i in (0, 1)], axis=0
        )
        start = jnp.zeros((256, 128), jnp.float32)
        start_row = jnp.zeros((2, 128), jnp.float32)
        for d in range(DOCS - 1):
            hits = jnp.sum(jnp.where(every == d, 1.0, 0.0), axis=0)
            held = jnp.sum(jnp.sum(hits, axis=0, keepdims=True), axis=1, keepdims=True)
            start = start + jnp.where(idc > d, held, 0.0)
            start_row = start_row + jnp.where(mine > d, held, 0.0)
        for i in (0, 1):
            for h in range(4):
                startr[0:1, h * 256 + i * 128 : h * 256 + (i + 1) * 128] = start_row[i : i + 1, :]
        row = lax.broadcasted_iota(jnp.int32, (256, 128), 0).astype(jnp.float32)
        tok = row + (seq * 256).astype(jnp.float32)
        angle = (tok - start) * freq_in[0:1, :]
        lane = lax.broadcasted_iota(jnp.int32, (256, 128), 1)
        cosb[...] = jnp.cos(angle)
        sinb[...] = jnp.where(lane < 64, -1.0, 1.0) * jnp.sin(angle)

    def normalise(p):
        total = squares(p, 1 - zhi, totals[p])
        factor = lax.rsqrt(jnp.sum(total, axis=1, keepdims=True) * (1.0 / 8192.0) + eps)
        factor = jnp.broadcast_to(factor, (128, 128))

        @pl.loop(0, 8)
        def _(k):
            g = gbuf[k // 2, k % 2].astype(jnp.float32)
            for i in range(8):
                h = hbuf[k, p, :, :, i * 128 : (i + 1) * 128].reshape(128, 128)
                lane = pl.multiple_of(((i // 2) % 2 * 4 + k // 2) * 256 + (i % 2) * 128, 128)
                nbuf[(k % 2) * 2 + i // 4, p * 128 : (p + 1) * 128, pl.ds(lane, 128)] = (
                    h.astype(jnp.float32) * factor * g[i : i + 1, :]
                ).astype(jnp.bfloat16)

    def keys_values(p):
        rows = slice(p * 128, (p + 1) * 128)

        sums = jnp.zeros((128, 256), jnp.float32)
        for b in range(4):
            w = abuf[:, :, b].reshape(2048, 256)
            sums = sums + jnp.dot(nbuf[b, rows, :], w, preferred_element_type=jnp.float32)
        kmine = turn(sums[:, 0:128], rows).astype(jnp.bfloat16)
        vmine = sums[:, 128:256].astype(jnp.bfloat16)
        kvbuf[c, x, zlo, p, 0] = kmine
        kvbuf[c, x, zlo, p, 1] = vmine
        cache_out[0, rows, :] = kmine
        cache_out[1, rows, :] = vmine

    def queries():
        for h in range(4):
            q = turn(acc_b[:, h * 128 : (h + 1) * 128])
            qbuf[:, h * 256 : (h + 1) * 256] = jnp.transpose(q).astype(jnp.bfloat16)

    scale = 128 ** (-0.5)

    def chunk(x_, b, first):
        base = ((x_ * 4 + b) * 512).astype(jnp.float32)
        keys = kvbuf[:, x_, b, :, 0].reshape(512, 128)
        vals = jnp.transpose(kvbuf[:, x_, b, :, 1].reshape(512, 128))
        key = lax.broadcasted_iota(jnp.int32, (512, 128), 0).astype(jnp.float32)
        key = jnp.concatenate([key] * 8, axis=1)
        seen = key >= startr[...] - base
        if first:
            here = lax.broadcasted_iota(jnp.int32, (1, 1024), 1) % 256 + c * 256
            seen = seen & (key <= here.astype(jnp.float32))
        s = jnp.dot(keys, qbuf[...], preferred_element_type=jnp.float32)
        s = jnp.where(seen, s, -1e30)
        new = jnp.max(s, axis=0, keepdims=True)
        if not first:
            old = m_ref[...]
            new = jnp.maximum(old, new)
        p = jnp.exp2((s - new) * (scale * log2_e))
        total = jnp.sum(p, axis=0, keepdims=True)
        part = jnp.dot(vals, p.astype(jnp.bfloat16), preferred_element_type=jnp.float32)
        if first:
            l_ref[...] = total
            o_ref[...] = part
        else:
            alpha = jnp.exp2((old - new) * (scale * log2_e))
            l_ref[...] = l_ref[...] * alpha + total
            o_ref[...] = o_ref[...] * alpha + part
        m_ref[...] = new

    def attend(r):
        if r == 0:
            KV.sib_wait(x, 0)
            chunk(x, zlo, True)
            return
        todo = []
        if 1 <= r <= 3:
            b = KV.block(r)
            KV.sib_wait(x, r)
            todo.append((x, b, b < zlo))
        if 1 <= r <= 4:
            KV.sib_wait(xm, r - 1)
            todo.append((x - 1, KV.block(r - 1), x >= 1))
        if 2 <= r <= 5:
            b = KV.block(r - 2)
            KV.sib_wait(xo, r - 2)
            todo.append((x - 2, b, (x >= 2) & (b >= zlo)))

        @pl.loop(0, len(todo))
        def _(i):
            x_, b, cond = todo[-1]
            for j in range(len(todo) - 1):
                x_ = jnp.where(i == j, todo[j][0], x_)
                b = jnp.where(i == j, todo[j][1], b)
                cond = ((i == j) & todo[j][2]) | ((i != j) & cond)

            @pl.when(cond)
            def _():
                chunk(x_, b, False)

    def finish():
        for h in range(4):
            lanes = slice(h * 256, (h + 1) * 256)
            att_out[:, h * 128 : (h + 1) * 128] = jnp.transpose(
                o_ref[:, lanes] / l_ref[0:1, lanes]
            ).astype(jnp.bfloat16)
            lse_out[h : h + 1, :] = m_ref[0:1, lanes] * scale + jnp.log(l_ref[0:1, lanes])

    acc_b[...] = jnp.zeros_like(acc_b)

    A.z_first(1)
    B.x_first(1)
    A.z_first(0)
    B.z_first(1)
    hy_send(1)
    hy_send(0)
    y_fwd(1, zhi, 1)
    small_two()
    A.x_first(0)
    B.x_first(0)
    B.x_fwd(0, 1)
    B.z_first(0)
    A.x_fwd(0, 0)
    hz_send(0)
    hz_send(1)
    A.z_step(1, 1)
    A.x_first(1)
    B.z_step(1, 1)
    A.z_step(1, 0)
    A.z_step(2, 0)
    A.opp_step(0, 0)
    A.x_fwd(2, 0)
    y_fwd(0, zhi, 0)
    B.x_fwd(0, 0)
    B.x_rest(0)
    relay(0)
    B.z_step(1, 0)
    B.x_fwd(1, 1)
    A.x_fwd(1, 0)
    A.x_rest(1)
    A.z_step(2, 1)
    A.x_fwd(1, 1)
    relay(1)
    B.x_fwd(1, 0)
    A.z_step(3, 0)
    y_end(0, zhi, 0)
    A.z_step(3, 1)
    A.opp_step(1, 1)
    A.opp_step(1, 0)
    cross(0)
    A.x_fwd(2, 1)
    small_three()
    A.opp_step(2, 0)
    B.z_step(2, 0)
    A.x_fwd(0, 1)
    cross(1)
    sib_all(A, 1)
    A.x_rest(2)
    A.x_fwd(3, 0)
    y_end(1, zhi, 1)
    B.opp_step(1, 0)
    own_squares()
    A.x_fwd(3, 1)
    B.z_step(2, 1)
    y_fwd(2, 1 - zhi, 0)
    B.z_step(3, 0)
    B.z_step(3, 1)
    B.opp_step(1, 1)
    A.opp_step(0, 1)
    A.x_rest(3)
    A.opp_step(3, 1)
    A.opp_step(2, 1)
    y_fwd(3, 1 - zhi, 1)
    tables()
    sib_all(A, 2)
    B.x_fwd(3, 0)
    A.opp_step(3, 0)
    A.x_rest(0)
    B.x_fwd(2, 1)
    sib_all(A, 0)
    sib_all(A, 3)
    y_end(2, 1 - zhi, 0)
    normalise(0)
    B.opp_step(0, 1)
    y_end(3, 1 - zhi, 1)
    keys_values(0)
    B.opp_step(0, 0)
    KV.z_first(0)
    B.x_fwd(2, 0)
    B.x_fwd(3, 1)
    normalise(1)
    B.x_rest(3)
    keys_values(1)
    B.x_rest(2)
    sib_all(B, 0)
    multiply(B, acc_b, nbuf, 0, 512)
    KV.x_first(0)
    KV.z_first(1)
    B.opp_step(3, 0)
    KV.x_first(1)
    B.opp_step(3, 1)
    B.x_rest(1)
    KV.z_step(2, 1)
    KV.z_step(2, 0)
    KV.z_step(1, 0)
    sib_all(B, 3)
    multiply(B, acc_b, nbuf, 3, 512)
    sib_all(B, 1)
    multiply(B, acc_b, nbuf, 1, 512)
    KV.x_fwd(0, 0)
    B.opp_step(2, 1)
    KV.z_step(1, 1)
    KV.x_fwd(2, 1)
    B.opp_step(2, 0)
    KV.x_fwd(0, 1)
    KV.z_step(3, 0)
    KV.x_fwd(1, 0)
    KV.x_rest(0)
    KV.opp_step(0, 1)
    KV.x_fwd(2, 0)
    KV.opp_step(2, 1)
    KV.x_fwd(1, 1)
    sib_all(B, 2)
    multiply(B, acc_b, nbuf, 2, 512)
    KV.z_step(3, 1)
    KV.opp_step(0, 0)
    queries()
    KV.x_rest(1)
    KV.x_rest(2)
    attend(0)
    KV.opp_step(1, 1)
    attend(2)
    KV.x_fwd(3, 1)
    KV.x_fwd(3, 0)
    KV.opp_step(1, 0)
    attend(1)
    KV.x_rest(3)
    KV.opp_step(2, 0)
    attend(3)
    KV.opp_step(3, 0)
    KV.opp_step(3, 1)
    attend(4)
    attend(5)
    finish()

    for cond, d in sent:
        if cond is None:
            d.wait_send()
        else:
            @pl.when(cond)
            def _(d=d):
                d.wait_send()


def put(*refs):
    for source, target in zip(refs[:3], refs[3:]):
        target[...] = source[...]


def on_device(hidden, gain, w_query, w_key, w_value, doc_ids):
    bf, f32 = jnp.bfloat16, jnp.float32
    hid = hidden.reshape(2, 2, 64, 1024)
    tile = doc_ids.reshape(2, 128)
    gains = gain.reshape(8, 128)
    freq = np.exp(np.arange(64, dtype=np.float32) * np.float32(-2.0 * log_theta / 128))
    freq = jnp.asarray(np.tile(np.concatenate([freq, freq])[None], (8, 1)).astype(np.float32))
    dma = pltpu.SemaphoreType.DMA
    any_, vm = pl.BlockSpec(memory_space=pl.ANY), pl.BlockSpec(memory_space=pltpu.VMEM)
    mixed, cache, sums = pl.pallas_call(
        fused,
        out_shape=(
            jax.ShapeDtypeStruct((256, 512), bf),
            jax.ShapeDtypeStruct((2, 256, 128), bf),
            jax.ShapeDtypeStruct((4, 256), f32),
        ),
        in_specs=[any_] * 6 + [vm],
        out_specs=(vm, vm, vm),
        scratch_shapes=[
            pltpu.VMEM((8, 2, 2, 64, 1024), bf),
            pltpu.VMEM((2, 2, 64, 1024), bf),
            pltpu.VMEM((4, 256, 2048), bf),
            pltpu.VMEM((2, 4, 4, 2, 128, 256), bf),
            pltpu.VMEM((2, 4, 4, 2, 128, 512), bf),
            pltpu.VMEM((2, 4, 4, 2, 2, 128, 128), bf),
            pltpu.VMEM((2, 4, 4, 2, 128), jnp.int32),
            pltpu.VMEM((4, 2, 8, 128), bf),
            pltpu.VMEM((256, 512), f32),
            pltpu.VMEM((128, 1024), bf),
            pltpu.VMEM((256, 128), f32),
            pltpu.VMEM((256, 128), f32),
            pltpu.VMEM((1, 1024), f32),
            pltpu.VMEM((1, 1024), f32),
            pltpu.VMEM((1, 1024), f32),
            pltpu.VMEM((128, 1024), f32),
            dma((6,)), dma((11,)), dma((11,)), dma((2, 2, 2)), dma((2, 2, 2)),
            dma((4, 2, 2)), dma((4, 2, 2)), dma((4, 2)), dma((4, 2)),
        ]
        + [
            dma((2, 4, 2)), dma((4, 2)), dma((2, 4, 2)), dma((2, 4, 2)),
            dma((2, 4)), dma((2, 4)), dma((4, 4, 2)), dma((4, 4, 2)),
        ] * 3,
        compiler_params=pltpu.CompilerParams(
            collective_id=0, has_side_effects=True, vmem_limit_bytes=62 * 1024 * 1024
        ),
        name="fused",
    )(
        hid, gains, w_query.reshape(2, 128, 512), w_key.reshape(2, 128, 128),
        w_value.reshape(2, 128, 128), tile, freq,
    )
    return pl.pallas_call(
        put,
        out_shape=tuple(jax.ShapeDtypeStruct(t.shape, t.dtype) for t in (mixed, cache, sums)),
        in_specs=[vm] * 3,
        out_specs=(vm,) * 3,
        name="put",
    )(mixed, cache, sums)


def solution(mesh):
    in_specs = (P("seq", "kv"), P("kv"), P("seq", "kv"), P("seq", "kv"), P("seq", "kv"), P("seq"))
    out_specs = (P("seq", "kv"), P(None, "seq", "kv"), P("kv", "seq"))
    return jax.shard_map(
        on_device, mesh=mesh, in_specs=in_specs, out_specs=out_specs, check_vma=False
    )
```
